32 devices in a mesh: snap: 16 (over z, y, x), vert: 2 (over core).
Axes of the slice: x: 2, y: 2, z: 4, core: 2. Of those that a mesh axis runs over, the one named last changes fastest.
Arguments:
- features: bfloat16 [32, 2048, 128], P('snap', 'vert'), may hold values from -6 to 6
- tile_cols: int32 [32, 16, 8], P('snap', 'vert'), may hold values from 0 to 15
- tile_weights: int32 [32, 16, 8, 128, 128], P('snap', 'vert'), may hold values from 0 to 3
- graph_gain: float32 [2, 128], replicated, may hold values from 0.5 to 1.5
- graph_up: bfloat16 [2, 128, 512], replicated, may hold values from -0.5 to 0.5
- graph_down: bfloat16 [2, 512, 128], replicated, may hold values from -0.25 to 0.25
- lag_mix: float32 [2, 8, 128], replicated, may hold values from -2 to 2
- time_gain: float32 [2, 128], replicated, may hold values from 0.5 to 1.5
- time_up: bfloat16 [2, 128, 1024], replicated, may hold values from -0.5 to 0.5
- time_down: bfloat16 [2, 1024, 128], replicated, may hold values from -0.1875 to 0.1875
Outputs:
- result: bfloat16 [32, 2048, 128], P('snap', 'vert')
The draws below stay inside these ranges and needn't reach their ends.
All inputs are finite; a program needn't handle non-finite values.
Results may differ from the reference program's by a relative error of at most 0.0085.
Values may be sent and summed in bfloat16 or wider, within the bound.
A program may use at most 64 MiB of HBM per device.

```python
import jax
import jax.numpy as jnp
from jax import lax

F = 128
HG = 512
HT = 1024
TILE = 128
K = 8
LAGS = 8
LAYERS = 2
SNAPS = 32
VERTS = 2048


def with_ends(drawn, stream_key, least, high):
    spot = [jax.random.randint(jax.random.fold_in(stream_key, axis), (), 0, length) for axis, length in enumerate(drawn.shape)]
    longest = drawn.shape.index(max(drawn.shape))
    neighbour = spot[:longest] + [(spot[longest] + 1) % drawn.shape[longest]] + spot[longest + 1:]
    return drawn.at[tuple(spot)].set(least).at[tuple(neighbour)].set(high)


def block_levels(rng, shape, split, low, high):
    def one(position, blocks):
        heights = jax.random.uniform(jax.random.fold_in(jax.random.fold_in(rng, 6), position), (blocks,), jnp.float32, low / len(split), high / len(split))
        return jnp.repeat(jnp.exp(heights), shape[position] // blocks).reshape((-1,) + (1,) * (len(shape) - position - 1))

    gain = one(*split[0])
    for cut in split[1:]:
        gain = gain * one(*cut)
    return gain


def gaussian(key, extent, scale, bound, pieces=(), held_as=jnp.bfloat16):
    drawn = jax.random.normal(key, extent, jnp.float32) * scale
    if len(pieces) > 0:
        drawn = block_levels(key, extent, pieces, -0.22, 0.18) * drawn
    return jnp.clip(drawn, min=-bound, max=bound).astype(held_as)


def setup_inputs(seed: int = 0) -> dict:
    key_of = jax.random.split(jax.random.key(seed), 11)
    features = gaussian(key_of[0], (SNAPS, VERTS, F), 1.0, 6.0, ((0, 16), (1, 2)))
    tile_cols = with_ends(jax.random.randint(key_of[1], (SNAPS, VERTS // TILE, K), 0, VERTS // TILE), jax.random.fold_in(key_of[1], 1), 0, (VERTS // TILE) - 1).astype(jnp.int32)
    tile_weights = with_ends(jax.random.randint(key_of[2], (SNAPS, VERTS // TILE, K, TILE, TILE), 0, 4), jax.random.fold_in(key_of[2], 1), 0, 3).astype(jnp.int32)
    graph_gain = jnp.clip(1.0 + 0.1 * jax.random.normal(key_of[3], (LAYERS, F), jnp.float32), 0.5, 1.5)
    graph_up = gaussian(key_of[4], (LAYERS, F, HG), F ** -0.5, 0.5)
    graph_down = gaussian(key_of[5], (LAYERS, HG, F), HG ** -0.5, 0.25)
    lag_mix = gaussian(key_of[6], (LAYERS, LAGS, F), LAGS ** -0.5, 2.0, (), jnp.float32)
    time_gain = jnp.clip(1.0 + 0.1 * jax.random.normal(key_of[7], (LAYERS, F), jnp.float32), 0.5, 1.5)
    time_up = gaussian(key_of[8], (LAYERS, F, HT), F ** -0.5, 0.5)
    time_down = gaussian(key_of[9], (LAYERS, HT, F), HT ** -0.5, 0.1875)
    return dict(features=features, tile_cols=tile_cols, tile_weights=tile_weights, graph_gain=graph_gain, graph_up=graph_up, graph_down=graph_down, lag_mix=lag_mix, time_gain=time_gain, time_up=time_up, time_down=time_down)


eps = 1e-06

def rms_scale(activation, gain_row):
    return activation * lax.rsqrt(lax.optimization_barrier(jnp.mean(activation * activation, axis=-1, keepdims=True)) + eps) * gain_row

def mlp_branch(residual, mixed_rows, gain_row, up_weight, down_weight):
    feature_width = residual.shape[-1]
    normed = rms_scale(mixed_rows, gain_row).astype(jnp.bfloat16).reshape(-1, feature_width)
    hidden = jax.nn.gelu(jnp.dot(normed, up_weight, preferred_element_type=jnp.float32)).astype(jnp.bfloat16)
    branch = jnp.dot(hidden, down_weight, preferred_element_type=jnp.float32).reshape(residual.shape)
    return (residual.astype(jnp.float32) + branch).astype(jnp.bfloat16)

def lagged(sequence, lag_rows, before, out_count):
    widened = sequence.astype(jnp.float32)
    running = jnp.zeros((out_count,) + sequence.shape[1:], jnp.float32)
    for lag_step in range(lag_rows.shape[0]):
        running = running + lag_rows[lag_step] * lax.slice_in_dim(widened, before - lag_step, before - lag_step + out_count, axis=0)
    return running

def aggregate(snapshot, columns, blocks):
    feature_width = snapshot.shape[-1]
    stacked = snapshot.reshape(-1, TILE, feature_width)
    picked = stacked[columns]
    product = jnp.einsum('rkij,rkjf->rif', blocks.astype(jnp.float32), picked.astype(jnp.float32))
    return product.reshape(-1, feature_width)

def reference(features, tile_cols, tile_weights, graph_gain, graph_up, graph_down, lag_mix, time_gain, time_up, time_down):
    state = features
    for layer_index in range(LAYERS):

        def one_snapshot(operands):
            return aggregate(operands[0], operands[1], operands[2])
        summed = lax.map(one_snapshot, (state, tile_cols, tile_weights))
        graph_out = mlp_branch(state, summed, graph_gain[layer_index], graph_up[layer_index], graph_down[layer_index])
        padded = jnp.concatenate([jnp.zeros((LAGS - 1,) + graph_out.shape[1:], jnp.bfloat16), graph_out], axis=0)
        mixed_rows = lagged(padded, lag_mix[layer_index], LAGS - 1, SNAPS)
        state = mlp_branch(graph_out, mixed_rows, time_gain[layer_index], time_up[layer_index], time_down[layer_index])
    return state
```

```python
import functools

import jax
import jax.numpy as jnp
from jax import lax
from jax.experimental import pallas as pl
from jax.experimental.pallas import tpu as pltpu
from jax.sharding import PartitionSpec as P

eps = 1e-06
MESH = pl.DeviceIdType.MESH
STRIP = 16


def normalise(rows, gain_row):
    scale = lax.rsqrt(jnp.mean(rows * rows, axis=-1, keepdims=True) + eps)
    return (rows * scale * gain_row).astype(jnp.bfloat16)


def mlp(normed, up_weight, down_weight):
    hidden = jnp.dot(normed, up_weight, preferred_element_type=jnp.float32)
    hidden = jax.nn.gelu(hidden.astype(jnp.bfloat16))
    return jnp.dot(hidden, down_weight, preferred_element_type=jnp.float32)


def kernel(
    owners, verts, group,
    feats, cols_far, weights, graph_gain_far, lag_mix_far, time_gain_far, graph_up_far, graph_down_far, time_up_far, time_down_far,
    out, *scratch,
):
    layers = lag_mix_far.shape[0]
    full = scratch[:layers]
    (
        raw, blocks, sent_graph, window, sent_time,
        graph_up, graph_down, time_up, time_down, own_sem, far_sem, raw_sem, first_send, first_recv,
        a_send, a_recv, z_send, z_recv, b_send, b_recv, v_send, v_recv, out_sem,
        cols, graph_gain, lag_mix, time_gain, small_sem,
    ) = scratch[layers:]
    snaps, tiles, tile, width = feats.shape
    picks = weights.shape[2]
    lags = lag_mix_far.shape[1]
    rows = window.shape[3]
    held = group * snaps
    unused = held - (lags - 1)
    groups = owners // group
    ahead_tiles = tiles
    delay = min(5, tiles - 1)

    me = lax.axis_index("snap")
    core = lax.axis_index("vert")
    slot = me % group
    plane = me // group
    base = me - slot
    first_tile = core * tiles

    def strip(owner):
        return pl.ds(pl.multiple_of(owner * rows, rows), rows)

    def far_copy(i, l):
        far, near = (
            (graph_up_far, graph_up), (graph_down_far, graph_down), (time_up_far, time_up), (time_down_far, time_down)
        )[i]
        return pltpu.make_async_copy(far.at[l], near.at[l], far_sem.at[i, l])

    def raw_copy(r):
        return pltpu.make_async_copy(weights.at[:, r], raw.at[:, r], raw_sem.at[r])

    smalls = [
        pltpu.make_async_copy(src, dst, small_sem.at[i])
        for i, (src, dst) in enumerate(
            [(cols_far, cols), (graph_gain_far, graph_gain), (lag_mix_far, lag_mix), (time_gain_far, time_gain)]
        )
    ]
    own_copy = pltpu.make_async_copy(feats, full[0].at[:, pl.ds(first_tile, tiles)], own_sem)
    barrier = pltpu.get_barrier_semaphore()
    for q in range(1, verts):
        pl.semaphore_signal(barrier, inc=1, device_id=(me, (core + q) % verts), device_id_type=MESH)
    for d in range(1, group):
        pl.semaphore_signal(barrier, inc=1, device_id=(base + (slot + d) % group, core), device_id_type=MESH)

    @pl.when(plane > 0)
    def _():
        pl.semaphore_signal(barrier, inc=1, device_id=(me - group, core), device_id_type=MESH)

    @pl.when(plane < groups - 1)
    def _():
        pl.semaphore_signal(barrier, inc=1, device_id=(me + group, core), device_id_type=MESH)

    own_copy.start()
    for copy in smalls:
        copy.start()
    raw_copy(0).start()
    for i in range(2):
        far_copy(i, 0).start()
    for r in range(1, tiles):
        raw_copy(r).start()
    for l in range(layers):
        for i in range(4):
            if l > 0 or i > 1:
                far_copy(i, l).start()

    @pl.when(plane == 0)
    def _():
        for l in range(layers):
            for r in range(tiles):
                window[l, r, 0:held] = jnp.zeros((held, rows, width), jnp.bfloat16)

    ahead = jnp.where(plane < groups - 1, 1, 0)
    behind = jnp.where(plane > 0, 1, 0)
    with jax.named_scope("barrier"):
        pl.semaphore_wait(barrier, group - 1 + verts - 1 + ahead + behind)

    def first_copy(q):
        return pltpu.make_async_remote_copy(
            src_ref=feats,
            dst_ref=full[0].at[:, pl.ds(first_tile, tiles)],
            send_sem=first_send.at[q],
            recv_sem=first_recv.at[q],
            device_id=(me, (core + q) % verts),
            device_id_type=MESH,
        )

    for q in range(1, verts):
        first_copy(q).start()

    def convert(r):
        raw_copy(r).wait()
        for t in range(snaps):
            blocks[t, r] = jnp.concatenate(
                [raw[t, r, k].astype(jnp.float32).astype(jnp.bfloat16) for k in range(picks)], axis=1
            )

    early = min(3, tiles)
    for r in range(early):
        with jax.named_scope(f"k{r}"):
            convert(r)

    with jax.named_scope("first"):
        for copy in smalls:
            copy.wait()
        own_copy.wait()
        for q in range(1, verts):
            first_copy(q).wait_recv()

    def a_copy(l, r, d):
        owner = (slot + d) % group
        return pltpu.make_async_remote_copy(
            src_ref=sent_graph.at[l, r, :, strip(owner)],
            dst_ref=window.at[l, r, pl.ds(held + slot * snaps, snaps)],
            send_sem=a_send.at[l, r],
            recv_sem=a_recv.at[l, r],
            device_id=(base + owner, core),
            device_id_type=MESH,
        )

    def a_all(l, r):
        part = window.at[l, r, pl.ds(0, (group - 1) * snaps)]
        return pltpu.make_async_remote_copy(
            src_ref=part, dst_ref=part, send_sem=a_send.at[l, r], recv_sem=a_recv.at[l, r],
            device_id=(base + (slot + 1) % group, core), device_id_type=MESH,
        )

    def z_copy(l, r, start, count):
        return pltpu.make_async_remote_copy(
            src_ref=window.at[l, r, pl.ds(held + start, count)],
            dst_ref=window.at[l, r, pl.ds(start, count)],
            send_sem=z_send.at[l, r],
            recv_sem=z_recv.at[l, r],
            device_id=(jnp.minimum(me + group, owners - 1), core),
            device_id_type=MESH,
        )

    def z_all(l, r):
        return z_copy(l, r, unused, held - unused)

    def z_origin(l, r, origin):
        if unused == 0:
            z_copy(l, r, origin * snaps, snaps).start()
            return

        @pl.when(origin == 0)
        def _():
            z_copy(l, r, unused, snaps - unused).start()

        @pl.when(origin > 0)
        def _():
            z_copy(l, r, origin * snaps, snaps).start()

    def b_copy(l, r, d):
        home = (slot + d) % group
        target = out.at[:, r] if l == layers - 1 else full[l + 1].at[:, first_tile + r]
        return pltpu.make_async_remote_copy(
            src_ref=sent_time.at[l, r, pl.ds(home * snaps, snaps)],
            dst_ref=target.at[:, strip(slot)],
            send_sem=b_send.at[l, r],
            recv_sem=b_recv.at[l, r],
            device_id=(base + home, core),
            device_id_type=MESH,
        )

    def out_copy(r):
        own = sent_time.at[layers - 1, r, pl.ds(slot * snaps, snaps)]
        return pltpu.make_async_copy(own, out.at[:, r, strip(slot)], out_sem.at[r])

    def b_all(l, r):
        part = sent_time.at[l, r, pl.ds(0, (group - 1) * snaps)]
        return pltpu.make_async_remote_copy(
            src_ref=part, dst_ref=part, send_sem=b_send.at[l, r], recv_sem=b_recv.at[l, r],
            device_id=(base + (slot + 1) % group, core), device_id_type=MESH,
        )

    def v_copy(l, r, q):
        piece = full[l + 1].at[:, first_tile + r]
        return pltpu.make_async_remote_copy(
            src_ref=piece,
            dst_ref=piece,
            send_sem=v_send.at[l, r, q],
            recv_sem=v_recv.at[l, r, q],
            device_id=(me, (core + q) % verts),
            device_id_type=MESH,
        )

    def graph_step(l, r):
        if l == 0 and r >= early:
            convert(r)
        sums = []
        for t in range(snaps):
            picked = jnp.concatenate([full[l][t, cols[t, r, k]] for k in range(picks)], axis=0)
            sums.append(jnp.dot(blocks[t, r], picked, preferred_element_type=jnp.float32))
        summed = jnp.concatenate(sums, axis=0)
        branch = mlp(normalise(summed, graph_gain[l:l + 1]), graph_up[l], graph_down[l])
        state = full[l][:, first_tile + r].astype(jnp.float32)
        sent_graph[l, r] = (state + branch.reshape(snaps, tile, width)).astype(jnp.bfloat16)
        for d in range(1, group):
            a_copy(l, r, d).start()
        window[l, r, pl.ds(held + slot * snaps, snaps)] = sent_graph[l, r, :, strip(slot)]
        if r < ahead_tiles:

            @pl.when(plane < groups - 1)
            def _():
                z_origin(l, r, slot)

    def forward(l, r):
        a_all(l, r).wait_recv()

        @pl.when(plane < groups - 1)
        def _():
            if r < ahead_tiles:
                for d in range(1, group):
                    z_origin(l, r, (slot + d) % group)
            else:
                z_all(l, r).start()

    def time_step(l, batch):
        for r in batch:

            @pl.when(plane > 0)
            def _():
                z_all(l, r).wait_recv()

        spots, mixes, states = [], [], []
        for r in batch:
            for top in range(0, rows, STRIP):
                span = slice(top, top + STRIP)
                seen = {i: window[l, r, i, span].astype(jnp.float32) for i in range(unused, 2 * held)}
                for i in range(held):
                    mixed = lag_mix[l, 0:1] * seen[held + i]
                    for m in range(1, lags):
                        mixed = mixed + lag_mix[l, m:m + 1] * seen[held + i - m]
                    spots.append((r, i, span))
                    mixes.append(mixed)
                    states.append(seen[held + i])
        branch = mlp(normalise(jnp.concatenate(mixes, axis=0), time_gain[l:l + 1]), time_up[l], time_down[l])
        result = (jnp.concatenate(states, axis=0) + branch).astype(jnp.bfloat16)
        for n, (r, i, span) in enumerate(spots):
            sent_time[l, r, i, span] = result[n * STRIP:(n + 1) * STRIP]
        for r in batch:
            for d in range(1, group):
                b_copy(l, r, d).start()
            if l == layers - 1:
                out_copy(r).start()
            else:
                own = sent_time[l, r, pl.ds(slot * snaps, snaps)]
                full[l + 1][:, first_tile + r, strip(slot)] = own

    def collect(l, r):
        b_all(l, r).wait_recv()
        if l < layers - 1:
            for q in range(1, verts):
                v_copy(l, r, q).start()

    for l in range(layers):
        for i in range(2):
            far_copy(i, l).wait()
        for r in range(tiles):
            with jax.named_scope(f"g{l}_{r}"):
                graph_step(l, r)
            if r >= delay:
                with jax.named_scope(f"f{l}_{r - delay}"):
                    forward(l, r - delay)
        for i in range(2, 4):
            far_copy(i, l).wait()
        passed = tiles - delay
        for r in range(tiles):
            while passed < tiles and passed <= delay + r:
                with jax.named_scope(f"f{l}_{passed}"):
                    forward(l, passed)
                passed += 1
            with jax.named_scope(f"t{l}_{r}"):
                time_step(l, [r])
        for r in range(tiles):
            with jax.named_scope(f"c{l}_{r}"):
                collect(l, r)
        if l < layers - 1:
            with jax.named_scope(f"v{l}"):
                for r in range(tiles):
                    for q in range(1, verts):
                        v_copy(l, r, q).wait_recv()

    with jax.named_scope("drain"):
        for q in range(1, verts):
            first_copy(q).wait_send()
        for r in range(tiles):
            out_copy(r).wait()
        for l in range(layers):
            for r in range(tiles):
                a_all(l, r).wait_send()
                b_all(l, r).wait_send()
                if l < layers - 1:
                    for q in range(1, verts):
                        v_copy(l, r, q).wait_send()

                @pl.when(plane < groups - 1)
                def _():
                    z_all(l, r).wait_send()


def on_device(owners, verts, features, tile_cols, tile_weights, graph_gain, graph_up, graph_down, lag_mix, time_gain, time_up, time_down):
    snaps, vert_dev, width = features.shape
    _, tiles, picks, tile, _ = tile_weights.shape
    layers, lags = lag_mix.shape[0], lag_mix.shape[1]
    group = -(-(lags - 1) // snaps)
    while owners % group or tile % (group * STRIP):
        group += 1
    rows = tile // group
    held = group * snaps
    bf16 = jnp.bfloat16
    dma = pltpu.SemaphoreType.DMA
    result = pl.pallas_call(
        functools.partial(kernel, owners, verts, group),
        out_shape=jax.ShapeDtypeStruct((snaps, tiles, tile, width), bf16),
        in_specs=[pl.BlockSpec(memory_space=pltpu.HBM)] * 10,
        out_specs=pl.BlockSpec(memory_space=pl.ANY),
        scratch_shapes=[pltpu.VMEM((snaps, verts * tiles, tile, width), bf16)] * layers + [
            pltpu.VMEM((snaps, tiles, picks, tile, tile), jnp.int32),
            pltpu.VMEM((snaps, tiles, tile, picks * tile), bf16),
            pltpu.VMEM((layers, tiles, snaps, tile, width), bf16),
            pltpu.VMEM((layers, tiles, 2 * held, rows, width), bf16),
            pltpu.VMEM((layers, tiles, held, rows, width), bf16),
            pltpu.VMEM(graph_up.shape, bf16),
            pltpu.VMEM(graph_down.shape, bf16),
            pltpu.VMEM(time_up.shape, bf16),
            pltpu.VMEM(time_down.shape, bf16),
            dma,
            dma((4, layers)),
            dma((tiles,)),
            dma((verts,)),
            dma((verts,)),
        ] + [dma((layers, tiles))] * 6 + [dma((layers, tiles, verts))] * 2 + [dma((tiles,))] + [
            pltpu.SMEM(tile_cols.shape, jnp.int32),
            pltpu.VMEM(graph_gain.shape, jnp.float32),
            pltpu.VMEM(lag_mix.shape, jnp.float32),
            pltpu.VMEM(time_gain.shape, jnp.float32),
            dma((4,)),
        ],
        compiler_params=pltpu.CompilerParams(
            collective_id=0, has_side_effects=True, vmem_limit_bytes=36 * 1024 * 1024
        ),
    )(
        *[pltpu.with_memory_space_constraint(array, pltpu.HBM) for array in (
            features.reshape(snaps, tiles, tile, width), tile_cols, tile_weights,
            graph_gain, lag_mix, time_gain, graph_up, graph_down, time_up, time_down,
        )]
    )
    return result.reshape(features.shape)


def solution(mesh):
    return jax.shard_map(
        functools.partial(on_device, mesh.shape["snap"], mesh.shape["vert"]),
        mesh=mesh,
        in_specs=(
            P("snap", "vert", None),
            P("snap", "vert", None),
            P("snap", "vert", None, None, None),
        ) + (P(),) * 7,
        out_specs=P("snap", "vert", None),
        check_vma=False,
    )
```

```python
import functools

import jax
import jax.numpy as jnp
from jax import lax
from jax.experimental import pallas as pl
from jax.experimental.pallas import tpu as pltpu
from jax.sharding import PartitionSpec as P

eps = 1e-06
MESH = pl.DeviceIdType.MESH
STRIP = 16
EARLY = 3
BEHIND = 4


def normalise(rows, gain_row):
    scale = lax.rsqrt(jnp.mean(rows * rows, axis=-1, keepdims=True) + eps)
    return (rows * scale * gain_row).astype(jnp.bfloat16)


def mlp(normed, up_weight, down_weight):
    hidden = jnp.dot(normed, up_weight, preferred_element_type=jnp.float32)
    hidden = jax.nn.gelu(hidden.astype(jnp.bfloat16))
    return jnp.dot(hidden, down_weight, preferred_element_type=jnp.float32)


def kernel(
    owners, verts, group,
    feats, cols_far, weights, graph_gain_far, lag_mix_far, time_gain_far, graph_up_far, graph_down_far, time_up_far, time_down_far,
    out, *scratch,
):
    layers = lag_mix_far.shape[0]
    full = scratch[:layers]
    (
        raw, blocks, sent_graph, window, sent_time,
        graph_up, graph_down, time_up, time_down, own_sem, far_sem, raw_sem, first_send, first_recv,
        a_send, a_recv, a_soon, cross_send, cross_recv, z_send, z_recv, b_send, b_recv, v_send, v_recv, out_sem,
        cols, graph_gain, lag_mix, time_gain, small_sem,
    ) = scratch[layers:]
    snaps, tiles, tile, width = feats.shape
    picks = weights.shape[2]
    lags = lag_mix_far.shape[1]
    rows = window.shape[3]
    held = group * snaps
    unused = held - (lags - 1)
    groups = owners // group
    early = min(EARLY, tiles)
    skip = min(unused, snaps - 1)

    me = lax.axis_index("snap")
    core = lax.axis_index("vert")
    slot = me % group
    plane = me // group
    base = me - slot
    first_tile = core * tiles

    def partner(d, back=False):
        if group == 4:
            return (slot + d) % 2 + 2 * ((slot // 2 + d // 2) % 2)
        return (slot + (group - d if back else d)) % group

    def strip(owner):
        return pl.ds(pl.multiple_of(owner * rows, rows), rows)

    def far_copy(i, l):
        far, near = (
            (graph_up_far, graph_up), (graph_down_far, graph_down), (time_up_far, time_up), (time_down_far, time_down)
        )[i]
        return pltpu.make_async_copy(far.at[l], near.at[l], far_sem.at[i, l])

    def raw_copy(r):
        return pltpu.make_async_copy(weights.at[:, r], raw.at[:, r], raw_sem.at[r])

    smalls = [
        pltpu.make_async_copy(src, dst, small_sem.at[i])
        for i, (src, dst) in enumerate(
            [(cols_far, cols), (graph_gain_far, graph_gain), (lag_mix_far, lag_mix), (time_gain_far, time_gain)]
        )
    ]
    own_copy = pltpu.make_async_copy(feats, full[0].at[:, pl.ds(first_tile, tiles)], own_sem)
    barrier = pltpu.get_barrier_semaphore()
    for q in range(verts):
        for d in range(group):
            if q + d > 0:
                pl.semaphore_signal(
                    barrier, inc=1, device_id=(base + partner(d), (core + q) % verts), device_id_type=MESH
                )

    @pl.when(plane > 0)
    def _():
        pl.semaphore_signal(barrier, inc=1, device_id=(me - group, core), device_id_type=MESH)

    @pl.when(plane < groups - 1)
    def _():
        pl.semaphore_signal(barrier, inc=1, device_id=(me + group, core), device_id_type=MESH)

    own_copy.start()
    for copy in smalls:
        copy.start()
    soon = min(2, tiles)
    for r in range(soon):
        raw_copy(r).start()
    for i in range(2):
        far_copy(i, 0).start()

    @pl.when(plane == 0)
    def _():
        for l in range(layers):
            for w in range(tiles):
                window[l, w, 0:held] = jnp.zeros((held, rows, width), jnp.bfloat16)

    ahead = jnp.where(plane < groups - 1, 1, 0)
    behind = jnp.where(plane > 0, 1, 0)
    with jax.named_scope("barrier"):
        pl.semaphore_wait(barrier, group * verts - 1 + ahead + behind)

    def first_copy(q):
        return pltpu.make_async_remote_copy(
            src_ref=feats,
            dst_ref=full[0].at[:, pl.ds(first_tile, tiles)],
            send_sem=first_send.at[q - 1],
            recv_sem=first_recv.at[q - 1],
            device_id=(me, (core + q) % verts),
            device_id_type=MESH,
        )

    for q in range(1, verts):
        first_copy(q).start()
    for r in range(soon, tiles):
        raw_copy(r).start()
    for l in range(layers):
        for i in range(4):
            if l > 0 or i > 1:
                far_copy(i, l).start()

    def convert(r):
        raw_copy(r).wait()
        for t in range(snaps):
            blocks[t, r] = jnp.concatenate(
                [raw[t, r, k].astype(jnp.float32).astype(jnp.bfloat16) for k in range(picks)], axis=1
            )

    with jax.named_scope("k0"):
        convert(0)

    with jax.named_scope("first"):
        for copy in smalls:
            copy.wait()
        own_copy.wait()
        for q in range(1, verts):
            first_copy(q).wait_recv()

    def remote(src, dst, send_sem, recv_sem, device):
        return pltpu.make_async_remote_copy(
            src_ref=src, dst_ref=dst, send_sem=send_sem, recv_sem=recv_sem, device_id=device, device_id_type=MESH
        )

    beside = (base + (slot + 1) % group, core)
    onward = (jnp.minimum(me + group, owners - 1), core)
    others = (group - 1) * snaps

    def a_copy(l, w, d):
        owner = partner(d)
        arrived = a_soon.at[l, w, d - 1] if w < early else a_recv.at[l, w]
        return remote(
            sent_graph.at[l, w, :, strip(owner)], window.at[l, w, pl.ds(held + slot * snaps, snaps)],
            a_send, arrived, (base + owner, core),
        )

    def a_all(l, w):
        part = window.at[l, w, pl.ds(0, others)]
        return remote(part, part, a_send, a_recv.at[l, w], beside)

    def z_copy(l, w, start, count):
        return remote(
            window.at[l, w, pl.ds(held + start, count)], window.at[l, w, pl.ds(start, count)],
            z_send, z_recv.at[l, w], onward,
        )

    def z_all(l, w):
        return z_copy(l, w, unused, held - unused)

    def z_origin(l, w, origin):
        if unused == 0:
            z_copy(l, w, origin * snaps, snaps).start()
            return

        @pl.when(origin == 0)
        def _():
            z_copy(l, w, skip, snaps - skip).start()

        @pl.when(origin > 0)
        def _():
            z_copy(l, w, origin * snaps, snaps).start()

    def b_mark(l, w):
        return l * tiles + w if l < layers - 1 else (layers - 1) * tiles

    def target(l, w):
        place = out.at[:, w] if l == layers - 1 else full[l + 1].at[:, first_tile + w]
        return place.at[:, strip(slot)]

    def b_copy(l, w, d):
        home = partner(d)
        return remote(
            sent_time.at[l, w, pl.ds(home * snaps, snaps)], target(l, w),
            b_send, b_recv.at[b_mark(l, w)], (base + home, core),
        )

    def cross_copy(l, d, q):
        home = partner(d)
        return remote(
            sent_time.at[l, tiles - 1, pl.ds(home * snaps, snaps)], target(l, tiles - 1),
            cross_send.at[l, q - 1], cross_recv.at[l, q - 1], (base + home, (core + q) % verts),
        )

    def cross_all(l, q):
        part = full[l + 1].at[:, first_tile + tiles - 1]
        return remote(part, part, cross_send.at[l, q - 1], cross_recv.at[l, q - 1], (me, (core + q) % verts))

    def b_all(l, w):
        part = sent_time.at[l, w, pl.ds(0, others)] if l < layers - 1 else sent_time.at[l, :, pl.ds(0, others)]
        return remote(part, part, b_send, b_recv.at[b_mark(l, w)], beside)

    def out_copy(w):
        own = sent_time.at[layers - 1, w, pl.ds(slot * snaps, snaps)]
        return pltpu.make_async_copy(own, out.at[:, w, strip(slot)], out_sem)

    def v_copy(l, part, q):
        return remote(part, part, v_send.at[l, q - 1], v_recv.at[l, q - 1], (me, (core + q) % verts))

    def v_all(l, q):
        return v_copy(l, full[l + 1].at[:, pl.ds(first_tile, tiles - 1)], q)

    def v_start(l, r):
        for q in range(1, verts):
            v_copy(l, full[l + 1].at[:, first_tile + r], q).start()

    def graph_step(l, r):
        if l == 0 and r > 0:
            convert(r)
        sums = []
        for t in range(snaps):
            picked = jnp.concatenate([full[l][t, cols[t, r, k]] for k in range(picks)], axis=0)
            sums.append(jnp.dot(blocks[t, r], picked, preferred_element_type=jnp.float32))
        summed = jnp.concatenate(sums, axis=0)
        branch = mlp(normalise(summed, graph_gain[l:l + 1]), graph_up[l], graph_down[l])
        state = full[l][:, first_tile + r].astype(jnp.float32)
        result = (state + branch.reshape(snaps, tile, width)).astype(jnp.bfloat16)
        sent_graph[l, r] = result
        for d in range(1, group):
            a_copy(l, r, d).start()
        window[l, r, pl.ds(held + slot * snaps, snaps)] = sent_graph[l, r, :, strip(slot)]

        @pl.when(plane < groups - 1)
        def _():
            z_origin(l, r, slot)

    def forward(l, w, parts):
        if w >= early:
            a_all(l, w).wait_recv()
        else:
            for d in parts:
                a_copy(l, w, d).wait_recv()

        @pl.when(plane < groups - 1)
        def _():
            for d in parts:
                z_origin(l, w, partner(d, True))

    def forward_most(l, w):
        forward(l, w, range(1, group - 1))

    def forward_last(l, w):
        forward(l, w, [group - 1])

    def forward_all(l, w):
        forward(l, w, range(1, group))

    def time_step(l, w):
        @pl.when(plane > 0)
        def _():
            z_all(l, w).wait_recv()

        spots, mixes, states = [], [], []
        for top in range(0, rows, STRIP):
            span = slice(top, top + STRIP)
            seen = {i: window[l, w, i, span].astype(jnp.float32) for i in range(unused, 2 * held)}
            for i in range(held):
                mixed = lag_mix[l, 0:1] * seen[held + i]
                for m in range(1, lags):
                    mixed = mixed + lag_mix[l, m:m + 1] * seen[held + i - m]
                spots.append((i, span))
                mixes.append(mixed)
                states.append(seen[held + i])
        branch = mlp(normalise(jnp.concatenate(mixes, axis=0), time_gain[l:l + 1]), time_up[l], time_down[l])
        result = (jnp.concatenate(states, axis=0) + branch).astype(jnp.bfloat16)
        for n, (i, span) in enumerate(spots):
            sent_time[l, w, i, span] = result[n * STRIP:(n + 1) * STRIP]
        for d in range(1, group):
            b_copy(l, w, d).start()
        if l < layers - 1 and w == tiles - 1:
            for q in range(1, verts):
                for d in range(group):
                    cross_copy(l, d, q).start()
        if l == layers - 1:
            out_copy(w).start()
        else:
            own = sent_time[l, w, pl.ds(slot * snaps, snaps)]
            full[l + 1][:, first_tile + w, strip(slot)] = own

    def collect(l, w):
        b_all(l, w).wait_recv()
        if w < tiles - 1:
            v_start(l, w)

    def run(kind, step, l, n):
        with jax.named_scope(f"{kind}{l}_{n}"):
            step(l, n)

    for l in range(layers):
        for i in range(2):
            far_copy(i, l).wait()
        for r in range(tiles):
            run("g", graph_step, l, r)
            w = r - BEHIND
            if 1 <= w <= early:
                run("fl", forward_last, l, w - 1)
            if 0 <= w < early:
                run("fm", forward_most, l, w)
        for i in range(2, 4):
            far_copy(i, l).wait()
        for w in range(max(tiles - BEHIND, 0), early):
            run("fm", forward_most, l, w)
        for w in range(max(tiles - BEHIND - 1, 0), early):
            run("fl", forward_last, l, w)
        passed = early
        for w in range(tiles):
            while passed < min(w + BEHIND, tiles):
                run("f", forward_all, l, passed)
                passed += 1
            run("t", time_step, l, w)
        if l < layers - 1:
            for w in range(tiles):
                run("c", collect, l, w)
            with jax.named_scope(f"v{l}"):
                for q in range(1, verts):
                    cross_all(l, q).wait_recv()
                    v_all(l, q).wait_recv()
        else:
            with jax.named_scope(f"c{l}"):
                b_all(l, 0).wait_recv()

    with jax.named_scope("drain"):
        for q in range(1, verts):
            first_copy(q).wait_send()
        part = out.at[:, :, pl.ds(0, rows)]
        pltpu.make_async_copy(part, part, out_sem).wait()
        part = window.at[:, :, pl.ds(0, others)]
        remote(part, part, a_send, a_recv.at[0, 0], beside).wait_send()
        part = sent_time.at[:, :, pl.ds(0, others)]
        remote(part, part, b_send, b_recv.at[0], beside).wait_send()
        for l in range(layers - 1):
            for q in range(1, verts):
                v_all(l, q).wait_send()
                cross_all(l, q).wait_send()

        @pl.when(plane < groups - 1)
        def _():
            part = window.at[:, :, pl.ds(unused, held - unused)]
            remote(part, part, z_send, z_recv.at[0, 0], onward).wait_send()


def on_device(owners, verts, features, tile_cols, tile_weights, graph_gain, graph_up, graph_down, lag_mix, time_gain, time_up, time_down):
    snaps, vert_dev, width = features.shape
    _, tiles, picks, tile, _ = tile_weights.shape
    layers, lags = lag_mix.shape[0], lag_mix.shape[1]
    group = -(-(lags - 1) // snaps)
    while owners % group or tile % (group * STRIP):
        group += 1
    rows = tile // group
    held = group * snaps
    bf16 = jnp.bfloat16
    dma = pltpu.SemaphoreType.DMA
    result = pl.pallas_call(
        functools.partial(kernel, owners, verts, group),
        out_shape=jax.ShapeDtypeStruct((snaps, tiles, tile, width), bf16),
        in_specs=[pl.BlockSpec(memory_space=pltpu.HBM)] * 10,
        out_specs=pl.BlockSpec(memory_space=pl.ANY),
        scratch_shapes=[pltpu.VMEM((snaps, verts * tiles, tile, width), bf16)] * layers + [
            pltpu.VMEM((snaps, tiles, picks, tile, tile), jnp.int32),
            pltpu.VMEM((snaps, tiles, tile, picks * tile), bf16),
            pltpu.VMEM((layers, tiles, snaps, tile, width), bf16),
            pltpu.VMEM((layers, tiles, 2 * held, rows, width), bf16),
            pltpu.VMEM((layers, tiles, held, rows, width), bf16),
            pltpu.VMEM(graph_up.shape, bf16),
            pltpu.VMEM(graph_down.shape, bf16),
            pltpu.VMEM(time_up.shape, bf16),
            pltpu.VMEM(time_down.shape, bf16),
            dma,
            dma((4, layers)),
            dma((tiles,)),
            dma((verts - 1,)),
            dma((verts - 1,)),
            dma,
            dma((layers, tiles)),
            dma((layers, min(EARLY, tiles), group - 1)),
            dma((layers - 1, verts - 1)),
            dma((layers - 1, verts - 1)),
            dma,
            dma((layers, tiles)),
            dma,
            dma(((layers - 1) * tiles + 1,)),
            dma((layers - 1, verts - 1)),
            dma((layers - 1, verts - 1)),
            dma,
            pltpu.SMEM(tile_cols.shape, jnp.int32),
            pltpu.VMEM(graph_gain.shape, jnp.float32),
            pltpu.VMEM(lag_mix.shape, jnp.float32),
            pltpu.VMEM(time_gain.shape, jnp.float32),
            dma((4,)),
        ],
        compiler_params=pltpu.CompilerParams(
            collective_id=0, has_side_effects=True, vmem_limit_bytes=36 * 1024 * 1024
        ),
    )(
        *[pltpu.with_memory_space_constraint(array, pltpu.HBM) for array in (
            features.reshape(snaps, tiles, tile, width), tile_cols, tile_weights,
            graph_gain, lag_mix, time_gain, graph_up, graph_down, time_up, time_down,
        )]
    )
    return result.reshape(features.shape)


def solution(mesh):
    return jax.shard_map(
        functools.partial(on_device, mesh.shape["snap"], mesh.shape["vert"]),
        mesh=mesh,
        in_specs=(
            P("snap", "vert", None),
            P("snap", "vert", None),
            P("snap", "vert", None, None, None),
        ) + (P(),) * 7,
        out_specs=P("snap", "vert", None),
        check_vma=False,
    )
```

```python
import functools

import jax
import jax.numpy as jnp
from jax import lax
from jax.experimental import pallas as pl
from jax.experimental.pallas import tpu as pltpu
from jax.sharding import PartitionSpec as P

eps = 1e-06
MESH = pl.DeviceIdType.MESH
STRIP = 16
EARLY = 3
SOONER = 8
CROSSING = 2
FIRST_CROSSING = 5
SIDEWAYS = 1
BEHIND = 4


def normalise(rows, gain_row):
    scale = lax.rsqrt(jnp.mean(rows * rows, axis=-1, keepdims=True) + eps)
    return (rows * scale * gain_row).astype(jnp.bfloat16)


def mlp(normed, up_weight, down_weight):
    hidden = jnp.dot(normed, up_weight, preferred_element_type=jnp.float32)
    hidden = jax.nn.gelu(hidden.astype(jnp.bfloat16))
    return jnp.dot(hidden, down_weight, preferred_element_type=jnp.float32)


def kernel(
    owners, verts, group,
    feats, cols_far, weights, graph_gain_far, lag_mix_far, time_gain_far, graph_up_far, graph_down_far, time_up_far, time_down_far,
    out, *scratch,
):
    layers = lag_mix_far.shape[0]
    full = scratch[:layers]
    (
        raw, blocks, sent_graph, window, sent_time, near, part_out, part_in, near_done,
        graph_up, graph_down, time_up, time_down, own_sem, far_sem, raw_sem, first_send, first_recv,
        a_send, a_recv, cross_send, cross_recv, z_send, z_recv, b_send, b_recv, v_send, v_recv, out_sem,
        nz_send, nz_recv, ny_send, ny_recv, nx_send, nx_recv, near_sem,
        cols, graph_gain, lag_mix, time_gain, small_sem,
    ) = scratch[layers:]
    snaps, tiles, tile, width = feats.shape
    picks = weights.shape[2]
    lags = lag_mix_far.shape[1]
    rows = window.shape[3]
    held = group * snaps
    unused = held - (lags - 1)
    groups = owners // group
    near_tiles = near_list(group, tiles)
    far_tiles = [r for r in range(tiles) if r not in near_tiles]
    apart, count = len(far_tiles), len(near_tiles)
    early = min(EARLY, apart)
    sooner = min(SOONER, apart)
    skip = min(unused, snaps - 1)

    me = lax.axis_index("snap")
    core = lax.axis_index("vert")
    slot = me % group
    plane = me // group
    base = me - slot
    first_tile = core * tiles
    slot_x, slot_y = slot % 2, slot // 2

    def partner(d, back=False):
        if group == 4:
            return (slot + d) % 2 + 2 * ((slot // 2 + d // 2) % 2)
        return (slot + (group - d if back else d)) % group

    def strip(owner):
        return pl.ds(pl.multiple_of(owner * rows, rows), rows)

    far_copies = [
        pltpu.make_async_copy(far, near, far_sem.at[i])
        for i, (far, near) in enumerate([
            (graph_up_far, graph_up), (graph_down_far, graph_down), (time_up_far, time_up), (time_down_far, time_down)
        ])
    ]
    loads = [(r, 1) for r in range(min(2, tiles))]
    while sum(loads[-1]) < tiles:
        loads.append((sum(loads[-1]), min(2, tiles - sum(loads[-1]))))

    def raw_copy(i):
        span = pl.ds(*loads[i])
        return pltpu.make_async_copy(weights.at[:, span], raw.at[:, span], raw_sem.at[i])

    smalls = [
        pltpu.make_async_copy(src, dst, small_sem.at[i])
        for i, (src, dst) in enumerate(
            [(cols_far, cols), (graph_gain_far, graph_gain), (lag_mix_far, lag_mix), (time_gain_far, time_gain)]
        )
    ]
    own_copy = pltpu.make_async_copy(feats, full[0].at[:, pl.ds(first_tile, tiles)], own_sem)
    barrier = pltpu.get_barrier_semaphore()
    for q in range(verts):
        for d in range(group):
            if q + d > 0:
                pl.semaphore_signal(
                    barrier, inc=1, device_id=(base + partner(d), (core + q) % verts), device_id_type=MESH
                )

    @pl.when(plane > 0)
    def _():
        pl.semaphore_signal(barrier, inc=1, device_id=(me - group, core), device_id_type=MESH)

    @pl.when(plane < groups - 1)
    def _():
        pl.semaphore_signal(barrier, inc=1, device_id=(me + group, core), device_id_type=MESH)

    own_copy.start()
    for copy in smalls:
        copy.start()
    for i in range(min(2, tiles)):
        raw_copy(i).start()
    for i in range(2):
        far_copies[i].start()

    @pl.when(plane == 0)
    def _():
        for l in range(layers):
            for w in range(apart):
                window[l, w, 0:held] = jnp.zeros((held, rows, width), jnp.bfloat16)
            for n in range(count):
                near[l, n, 0:snaps] = jnp.zeros((snaps, tile, width), jnp.bfloat16)

    ahead = jnp.where(plane < groups - 1, 1, 0)
    behind = jnp.where(plane > 0, 1, 0)
    with jax.named_scope("barrier"):
        pl.semaphore_wait(barrier, group * verts - 1 + ahead + behind)

    def first_copy(q):
        return pltpu.make_async_remote_copy(
            src_ref=feats,
            dst_ref=full[0].at[:, pl.ds(first_tile, tiles)],
            send_sem=first_send.at[q - 1],
            recv_sem=first_recv.at[q - 1],
            device_id=(me, (core + q) % verts),
            device_id_type=MESH,
        )

    for q in range(1, verts):
        first_copy(q).start()
    for i in range(min(2, tiles), len(loads)):
        raw_copy(i).start()
    for i in range(2, 4):
        far_copies[i].start()

    def convert(r):
        for i, (first, _) in enumerate(loads):
            if first == r:
                raw_copy(i).wait()
        for t in range(snaps):
            blocks[t, r] = jnp.concatenate(
                [raw[t, r, k].astype(jnp.float32).astype(jnp.bfloat16) for k in range(picks)], axis=1
            )

    with jax.named_scope("k0"):
        convert(0)

    with jax.named_scope("first"):
        for copy in smalls:
            copy.wait()
        own_copy.wait()
        for q in range(1, verts):
            first_copy(q).wait_recv()

    def remote(src, dst, send_sem, recv_sem, device):
        return pltpu.make_async_remote_copy(
            src_ref=src, dst_ref=dst, send_sem=send_sem, recv_sem=recv_sem, device_id=device, device_id_type=MESH
        )

    beside = (base + (slot + 1) % group, core)
    onward = (jnp.minimum(me + group, owners - 1), core)
    others = (group - 1) * snaps

    def a_mark(w, d):
        return 2 * w + (1 if d == group - 1 else 0) if w < early else w + early

    def a_copy(l, w, d):
        owner = partner(d)
        return remote(
            sent_graph.at[l, w, :, strip(owner)], window.at[l, w, pl.ds(held + slot * snaps, snaps)],
            a_send, a_recv.at[a_mark(w, d)], (base + owner, core),
        )

    def a_some(l, w, count, d):
        part = window.at[l, w, pl.ds(0, count * snaps)]
        return remote(part, part, a_send, a_recv.at[a_mark(w, d)], beside)

    def z_copy(l, w, start, count):
        return remote(
            window.at[l, w, pl.ds(held + start, count)], window.at[l, w, pl.ds(start, count)],
            z_send, z_recv.at[l, w], onward,
        )

    def z_all(l, w):
        return z_copy(l, w, unused, held - unused)

    def z_origin(l, w, origin):
        if unused == 0:
            z_copy(l, w, origin * snaps, snaps).start()
            return

        @pl.when(origin == 0)
        def _():
            z_copy(l, w, skip, snaps - skip).start()

        @pl.when(origin > 0)
        def _():
            z_copy(l, w, origin * snaps, snaps).start()

    def b_mark(l, w):
        return l * apart + w if l < layers - 1 else (layers - 1) * apart

    def target(l, w):
        r = far_tiles[w]
        place = out.at[:, r] if l == layers - 1 else full[l + 1].at[:, first_tile + r]
        return place.at[:, strip(slot)]

    def b_copy(l, w, d):
        home = partner(d)
        return remote(
            sent_time.at[l, w, pl.ds(home * snaps, snaps)], target(l, w),
            b_send, b_recv.at[b_mark(l, w)], (base + home, core),
        )

    def cross_copy(l, d, q):
        home = partner(d)
        return remote(
            sent_time.at[l, apart - 1, pl.ds(home * snaps, snaps)], target(l, apart - 1),
            cross_send.at[l, q - 1], cross_recv.at[l, q - 1], (base + home, (core + q) % verts),
        )

    def cross_all(l, q):
        part = full[l + 1].at[:, first_tile + tiles - 1]
        return remote(part, part, cross_send.at[l, q - 1], cross_recv.at[l, q - 1], (me, (core + q) % verts))

    def b_all(l, w):
        part = sent_time.at[l, w, pl.ds(0, others)] if l < layers - 1 else sent_time.at[l, :, pl.ds(0, others)]
        return remote(part, part, b_send, b_recv.at[b_mark(l, w)], beside)

    def out_copy(w):
        own = sent_time.at[layers - 1, w, pl.ds(slot * snaps, snaps)]
        return pltpu.make_async_copy(own, out.at[:, far_tiles[w], strip(slot)], out_sem)

    def v_copy(l, part, q):
        return remote(part, part, v_send.at[l, q - 1], v_recv.at[l, q - 1], (me, (core + q) % verts))

    def v_all(l, q):
        return v_copy(l, full[l + 1].at[:, pl.ds(first_tile, tiles - 1)], q)

    def v_start(l, r):
        for q in range(1, verts):
            v_copy(l, full[l + 1].at[:, first_tile + r], q).start()

    def nz_copy(l, n, first):
        return remote(
            near.at[l, n, pl.ds(2 * snaps + first, snaps - first)], near.at[l, n, pl.ds(first, snaps - first)],
            nz_send, nz_recv.at[l, n], onward,
        )

    def nz_do(act):
        if skip == 0:
            act(0)
            return

        @pl.when(slot == 0)
        def _():
            act(skip)

        @pl.when(slot > 0)
        def _():
            act(0)

    def ny_copy(l, n):
        return remote(
            near.at[l, n, pl.ds(2 * snaps * (1 - slot_y), snaps)], near.at[l, n, pl.ds(snaps, snaps)],
            ny_send, ny_recv.at[l, n], (base + (slot + 2) % group, core),
        )

    def nx_copy(l, n):
        return remote(
            part_out.at[l, n], part_in.at[l, n], nx_send, nx_recv.at[l, n], (base + slot + 1 - 2 * slot_x, core)
        )

    def lag_sum(l, i, sources):
        total = None
        for apart_by, values in sources:
            for j in range(snaps):
                lag = apart_by * snaps + i - j
                if 0 <= lag < lags:
                    term = lag_mix[l, lag:lag + 1] * values[j]
                    total = term if total is None else total + term
        return total

    def near_load(l, n, first, span):
        return [near[l, n, first + j, span].astype(jnp.float32) for j in range(snaps)]

    def near_y(l, n):
        @pl.when(slot_y == 1)
        def _():
            @pl.when(plane > 0)
            def _():
                nz_do(lambda first: nz_copy(l, n, first).wait_recv())

            ny_copy(l, n).start()

        @pl.when(slot_y == 0)
        def _():
            ny_copy(l, n).start()

    def near_x(l, n):
        @pl.when((slot_y == 0) & (plane > 0))
        def _():
            nz_do(lambda first: nz_copy(l, n, first).wait_recv())

        ny_copy(l, n).wait_recv()
        for top in range(0, tile, STRIP):
            span = slice(top, top + STRIP)
            newer = near_load(l, n, snaps * (2 - slot_x), span)
            older = near_load(l, n, snaps * (1 - slot_x), span)
            for i in range(snaps):
                part_out[l, n, i, span] = lag_sum(l, i, [(1, newer), (3, older)]).astype(jnp.bfloat16)
        nx_copy(l, n).start()

    def near_time(l, n):
        r = near_tiles[n]
        nx_copy(l, n).wait_recv()
        spots, mixes, states = [], [], []
        for top in range(0, tile, STRIP):
            span = slice(top, top + STRIP)
            seen = [near_load(l, n, snaps * p, span) for p in range(3)]
            for i in range(snaps):
                mixed = lag_sum(l, i, [(0, seen[2]), (2, seen[1]), (4, seen[0])])
                mixes.append(mixed + part_in[l, n, i, span].astype(jnp.float32))
                states.append(seen[2][i])
                spots.append((i, span))
        branch = mlp(normalise(jnp.concatenate(mixes, axis=0), time_gain[l:l + 1]), time_up[l], time_down[l])
        result = (jnp.concatenate(states, axis=0) + branch).astype(jnp.bfloat16)
        for k, (i, span) in enumerate(spots):
            piece = result[k * STRIP:(k + 1) * STRIP]
            if l == layers - 1:
                near_done[n, i, span] = piece
            else:
                full[l + 1][i, first_tile + r, span] = piece
        if l == layers - 1:
            near_out(n).start()
        else:
            v_start(l, r)

    def near_out(n):
        return pltpu.make_async_copy(near_done.at[n], out.at[:, near_tiles[n]], near_sem)

    def graph_step(l, r):
        if l == 0 and r > 0:
            convert(r)
        sums = []
        for t in range(snaps):
            picked = jnp.concatenate([full[l][t, cols[t, r, k]] for k in range(picks)], axis=0)
            sums.append(jnp.dot(blocks[t, r], picked, preferred_element_type=jnp.float32))
        summed = jnp.concatenate(sums, axis=0)
        branch = mlp(normalise(summed, graph_gain[l:l + 1]), graph_up[l], graph_down[l])
        state = full[l][:, first_tile + r].astype(jnp.float32)
        result = (state + branch.reshape(snaps, tile, width)).astype(jnp.bfloat16)
        if r in near_tiles:
            n = near_tiles.index(r)
            near[l, n, 2 * snaps:3 * snaps] = result

            @pl.when(plane < groups - 1)
            def _():
                nz_do(lambda first: nz_copy(l, n, first).start())

            return
        w = far_tiles.index(r)
        sent_graph[l, w] = result
        for d in range(1, group) if w < early else reversed(range(1, group)):
            a_copy(l, w, d).start()
        window[l, w, pl.ds(held + slot * snaps, snaps)] = sent_graph[l, w, :, strip(slot)]

        if w < sooner:

            @pl.when(plane < groups - 1)
            def _():
                z_origin(l, w, slot)

    def forward(l, w, parts):
        a_some(l, w, len(parts), parts[-1]).wait_recv()

        @pl.when(plane < groups - 1)
        def _():
            if w < sooner:
                for d in parts:
                    z_origin(l, w, partner(d, True))
            else:
                z_all(l, w).start()

    def forward_most(l, w):
        forward(l, w, range(1, group - 1))

    def forward_last(l, w):
        forward(l, w, [group - 1])

    def forward_all(l, w):
        forward(l, w, range(1, group))

    def time_step(l, w):
        @pl.when(plane > 0)
        def _():
            z_all(l, w).wait_recv()

        spots, mixes, states = [], [], []
        for top in range(0, rows, STRIP):
            span = slice(top, top + STRIP)
            seen = {i: window[l, w, i, span].astype(jnp.float32) for i in range(unused, 2 * held)}
            for i in range(held):
                mixed = lag_mix[l, 0:1] * seen[held + i]
                for m in range(1, lags):
                    mixed = mixed + lag_mix[l, m:m + 1] * seen[held + i - m]
                spots.append((i, span))
                mixes.append(mixed)
                states.append(seen[held + i])
        branch = mlp(normalise(jnp.concatenate(mixes, axis=0), time_gain[l:l + 1]), time_up[l], time_down[l])
        result = (jnp.concatenate(states, axis=0) + branch).astype(jnp.bfloat16)
        for n, (i, span) in enumerate(spots):
            sent_time[l, w, i, span] = result[n * STRIP:(n + 1) * STRIP]
        for d in reversed(range(1, group)):
            b_copy(l, w, d).start()
            if l < layers - 1 and w == apart - 1:
                for q in range(1, verts):
                    cross_copy(l, d, q).start()
        if l < layers - 1 and w == apart - 1:
            for q in range(1, verts):
                cross_copy(l, 0, q).start()
        if l == layers - 1:
            out_copy(w).start()
        else:
            own = sent_time[l, w, pl.ds(slot * snaps, snaps)]
            full[l + 1][:, first_tile + far_tiles[w], strip(slot)] = own

    def collect(l, w):
        b_all(l, w).wait_recv()
        if w < apart - 1:
            v_start(l, far_tiles[w])

    def run(kind, step, l, n):
        with jax.named_scope(f"{kind}{l}_{n}"):
            step(l, n)

    for l in range(layers):
        if l == 0:
            for i in range(2):
                far_copies[i].wait()
        ready = {}
        for w in range(early):
            ready.setdefault(min(far_tiles[w] + BEHIND + 1, tiles - 1), []).append(("fl", forward_last, w))
            ready.setdefault(min(far_tiles[w] + BEHIND, tiles - 1), []).append(("fm", forward_most, w))
        for r in range(tiles):
            run("g", graph_step, l, r)
            if r == tiles - SIDEWAYS:
                for n in range(count):
                    run("y", near_y, l, n)
            for kind, step, w in sorted(ready.get(r, []), key=lambda item: (item[2], item[0] == "fl")):
                run(kind, step, l, w)
        if l == 0:
            for i in range(2, 4):
                far_copies[i].wait()
        passed = early
        for w in range(apart):
            while passed < min(w + BEHIND, apart):
                run("f", forward_all, l, passed)
                passed += 1
            run("t", time_step, l, w)
            for n in range(count):
                if w == min(CROSSING, apart - 1):

                    @pl.when(plane > 0)
                    def _():
                        run("x", near_x, l, n)

                if w == min(FIRST_CROSSING, apart - 1):

                    @pl.when(plane == 0)
                    def _():
                        run("x", near_x, l, n)

        for n in range(count):
            run("n", near_time, l, n)
        if l < layers - 1:
            for w in range(apart):
                run("c", collect, l, w)
            with jax.named_scope(f"v{l}"):
                for q in range(1, verts):
                    cross_all(l, q).wait_recv()
                    v_all(l, q).wait_recv()
        else:
            with jax.named_scope(f"c{l}"):
                b_all(l, 0).wait_recv()

    with jax.named_scope("drain"):
        for q in range(1, verts):
            first_copy(q).wait_send()
        part = out.at[:, pl.ds(0, apart), pl.ds(0, rows)]
        pltpu.make_async_copy(part, part, out_sem).wait()
        part = window.at[:, :, pl.ds(0, others)]
        remote(part, part, a_send, a_recv.at[0], beside).wait_send()
        part = sent_time.at[:, :, pl.ds(0, others)]
        remote(part, part, b_send, b_recv.at[0], beside).wait_send()
        for l in range(layers - 1):
            for q in range(1, verts):
                v_all(l, q).wait_send()
                cross_all(l, q).wait_send()

        @pl.when(plane < groups - 1)
        def _():
            part = window.at[:, :, pl.ds(unused, held - unused)]
            remote(part, part, z_send, z_recv.at[0, 0], onward).wait_send()

        if count > 0:
            part = out.at[:, pl.ds(0, count)]
            pltpu.make_async_copy(part, part, near_sem).wait()
            part = near.at[:, :, pl.ds(0, snaps)]
            remote(part, part, ny_send, ny_recv.at[0, 0], beside).wait_send()
            remote(part_out, part_out, nx_send, nx_recv.at[0, 0], beside).wait_send()

            @pl.when(plane < groups - 1)
            def _():
                def take(first):
                    part = near.at[:, :, pl.ds(first, snaps - first)]
                    remote(part, part, nz_send, nz_recv.at[0, 0], onward).wait_send()

                nz_do(take)


def near_list(group, tiles):
    return [1] if group == 4 and tiles > 4 else []


def on_device(owners, verts, features, tile_cols, tile_weights, graph_gain, graph_up, graph_down, lag_mix, time_gain, time_up, time_down):
    snaps, vert_dev, width = features.shape
    _, tiles, picks, tile, _ = tile_weights.shape
    layers, lags = lag_mix.shape[0], lag_mix.shape[1]
    group = -(-(lags - 1) // snaps)
    while owners % group or tile % (group * STRIP):
        group += 1
    rows = tile // group
    held = group * snaps
    near_count = len(near_list(group, tiles))
    apart, count = tiles - near_count, max(near_count, 1)
    bf16 = jnp.bfloat16
    dma = pltpu.SemaphoreType.DMA
    result = pl.pallas_call(
        functools.partial(kernel, owners, verts, group),
        out_shape=jax.ShapeDtypeStruct((snaps, tiles, tile, width), bf16),
        in_specs=[pl.BlockSpec(memory_space=pltpu.HBM)] * 10,
        out_specs=pl.BlockSpec(memory_space=pl.ANY),
        scratch_shapes=[pltpu.VMEM((snaps, verts * tiles, tile, width), bf16)] * layers + [
            pltpu.VMEM((snaps, tiles, picks, tile, tile), jnp.int32),
            pltpu.VMEM((snaps, tiles, tile, picks * tile), bf16),
            pltpu.VMEM((layers, apart, snaps, tile, width), bf16),
            pltpu.VMEM((layers, apart, 2 * held, rows, width), bf16),
            pltpu.VMEM((layers, apart, held, rows, width), bf16),
            pltpu.VMEM((layers, count, 3 * snaps, tile, width), bf16),
            pltpu.VMEM((layers, count, snaps, tile, width), bf16),
            pltpu.VMEM((layers, count, snaps, tile, width), bf16),
            pltpu.VMEM((count, snaps, tile, width), bf16),
            pltpu.VMEM(graph_up.shape, bf16),
            pltpu.VMEM(graph_down.shape, bf16),
            pltpu.VMEM(time_up.shape, bf16),
            pltpu.VMEM(time_down.shape, bf16),
            dma,
            dma((4,)),
            dma((tiles,)),
            dma((verts - 1,)),
            dma((verts - 1,)),
            dma,
            dma((apart + min(EARLY, apart),)),
            dma((layers - 1, verts - 1)),
            dma((layers - 1, verts - 1)),
            dma,
            dma((layers, apart)),
            dma,
            dma(((layers - 1) * apart + 1,)),
            dma((layers - 1, verts - 1)),
            dma((layers - 1, verts - 1)),
            dma,
        ] + [dma, dma((layers, count))] * 3 + [
            dma,
            pltpu.SMEM(tile_cols.shape, jnp.int32),
            pltpu.VMEM(graph_gain.shape, jnp.float32),
            pltpu.VMEM(lag_mix.shape, jnp.float32),
            pltpu.VMEM(time_gain.shape, jnp.float32),
            dma((4,)),
        ],
        compiler_params=pltpu.CompilerParams(
            collective_id=0, has_side_effects=True, vmem_limit_bytes=36 * 1024 * 1024
        ),
    )(
        *[pltpu.with_memory_space_constraint(array, pltpu.HBM) for array in (
            features.reshape(snaps, tiles, tile, width), tile_cols, tile_weights,
            graph_gain, lag_mix, time_gain, graph_up, graph_down, time_up, time_down,
        )]
    )
    return result.reshape(features.shape)


def solution(mesh):
    return jax.shard_map(
        functools.partial(on_device, mesh.shape["snap"], mesh.shape["vert"]),
        mesh=mesh,
        in_specs=(
            P("snap", "vert", None),
            P("snap", "vert", None),
            P("snap", "vert", None, None, None),
        ) + (P(),) * 7,
        out_specs=P("snap", "vert", None),
        check_vma=False,
    )
```

```python
import functools

import jax
import jax.numpy as jnp
from jax import lax
from jax.experimental import pallas as pl
from jax.experimental.pallas import tpu as pltpu
from jax.sharding import PartitionSpec as P

eps = 1e-06
MESH = pl.DeviceIdType.MESH
STRIP = 16
GELU_A = 0.7978845608028654
GELU_B = GELU_A * 0.044715
EARLY = 3
SOONER = 8
CROSSING = 2
FIRST_CROSSING = 4
SIDEWAYS = 1
BEHIND = 4


def normalise(rows, gain_row):
    scale = lax.rsqrt(jnp.mean(rows * rows, axis=-1, keepdims=True) + eps)
    return (rows * scale * gain_row).astype(jnp.bfloat16)


def mlp(normed, up_weight, down_weight):
    hidden = jnp.dot(normed, up_weight, preferred_element_type=jnp.float32)
    hidden = hidden.astype(jnp.bfloat16)
    inner = hidden * (GELU_A + GELU_B * (hidden * hidden))
    half = hidden * 0.5
    hidden = half + half * jnp.tanh(inner)
    return jnp.dot(hidden, down_weight, preferred_element_type=jnp.float32)


def kernel(
    owners, verts, group,
    feats, cols_far, weights, graph_gain_far, lag_mix_far, time_gain_far, graph_up_far, graph_down_far, time_up_far, time_down_far,
    out, *scratch,
):
    layers = lag_mix_far.shape[0]
    full = scratch[:layers]
    (
        raw, blocks, sent_graph, window, sent_time, near, part_out, part_in, near_done,
        graph_up, graph_down, time_up, time_down, own_sem, far_sem, raw_sem, first_send, first_recv,
        a_send, a_recv, cross_send, cross_recv, z_send, z_recv, z_late, b_send, b_recv, v_send, v_recv, out_sem,
        nz_send, nz_recv, ny_send, ny_recv, nx_send, nx_recv, near_sem,
        cols, graph_gain, lag_mix, time_gain, small_sem,
    ) = scratch[layers:]
    snaps, tiles, tile, width = feats.shape
    picks = weights.shape[2]
    lags = lag_mix_far.shape[1]
    rows = window.shape[3]
    held = group * snaps
    unused = held - (lags - 1)
    groups = owners // group
    near_tiles = near_list(group, tiles)
    far_tiles = [r for r in range(tiles) if r not in near_tiles]
    apart, count = len(far_tiles), len(near_tiles)
    early = min(EARLY, apart)
    halved = [apart - 1] if rows % (2 * STRIP) == 0 and apart > early else []
    sooner = min(SOONER, apart - len(halved))
    skip = min(unused, snaps - 1)

    me = lax.axis_index("snap")
    core = lax.axis_index("vert")
    slot = me % group
    plane = me // group
    base = me - slot
    first_tile = core * tiles
    slot_x, slot_y = slot % 2, slot // 2

    def partner(d, back=False):
        if group == 4:
            return (slot + d) % 2 + 2 * ((slot // 2 + d // 2) % 2)
        return (slot + (group - d if back else d)) % group

    def strip(owner):
        return pl.ds(pl.multiple_of(owner * rows, rows), rows)

    far_copies = [
        pltpu.make_async_copy(far, near, far_sem.at[i])
        for i, (far, near) in enumerate([
            (graph_up_far, graph_up), (graph_down_far, graph_down), (time_up_far, time_up), (time_down_far, time_down)
        ])
    ]
    loads = [(r, 1) for r in range(min(2, tiles))]
    while sum(loads[-1]) < tiles:
        loads.append((sum(loads[-1]), min(2, tiles - sum(loads[-1]))))

    def raw_copy(i):
        span = pl.ds(*loads[i])
        return pltpu.make_async_copy(weights.at[:, span], raw.at[:, span], raw_sem.at[i])

    smalls = [
        pltpu.make_async_copy(src, dst, small_sem.at[i])
        for i, (src, dst) in enumerate(
            [(cols_far, cols), (graph_gain_far, graph_gain), (lag_mix_far, lag_mix), (time_gain_far, time_gain)]
        )
    ]
    own_copy = pltpu.make_async_copy(feats, full[0].at[:, pl.ds(first_tile, tiles)], own_sem)
    barrier = pltpu.get_barrier_semaphore()
    for q in range(verts):
        for d in range(group):
            if q + d > 0:
                pl.semaphore_signal(
                    barrier, inc=1, device_id=(base + partner(d), (core + q) % verts), device_id_type=MESH
                )

    @pl.when(plane > 0)
    def _():
        pl.semaphore_signal(barrier, inc=1, device_id=(me - group, core), device_id_type=MESH)

    @pl.when(plane < groups - 1)
    def _():
        pl.semaphore_signal(barrier, inc=1, device_id=(me + group, core), device_id_type=MESH)

    own_copy.start()
    for copy in smalls:
        copy.start()
    raw_copy(0).start()

    @pl.when(plane == 0)
    def _():
        for l in range(layers):
            for w in range(apart):
                window[l, w, 0:held] = jnp.zeros((held, rows, width), jnp.bfloat16)
            for n in range(count):
                near[l, n, 0:snaps] = jnp.zeros((snaps, tile, width), jnp.bfloat16)

    ahead = jnp.where(plane < groups - 1, 1, 0)
    behind = jnp.where(plane > 0, 1, 0)
    with jax.named_scope("barrier"):
        pl.semaphore_wait(barrier, group * verts - 1 + ahead + behind)

    def first_copy(q):
        return pltpu.make_async_remote_copy(
            src_ref=feats,
            dst_ref=full[0].at[:, pl.ds(first_tile, tiles)],
            send_sem=first_send.at[q - 1],
            recv_sem=first_recv.at[q - 1],
            device_id=(me, (core + q) % verts),
            device_id_type=MESH,
        )

    for q in range(1, verts):
        first_copy(q).start()
    for i in range(2):
        far_copies[i].start()
    for i in range(1, len(loads)):
        raw_copy(i).start()
    for i in range(2, 4):
        far_copies[i].start()

    def convert(r):
        for i, (first, _) in enumerate(loads):
            if first == r:
                raw_copy(i).wait()
        for t in range(snaps):
            blocks[t, r] = jnp.concatenate(
                [raw[t, r, k].astype(jnp.float32).astype(jnp.bfloat16) for k in range(picks)], axis=1
            )

    with jax.named_scope("k0"):
        convert(0)

    with jax.named_scope("first"):
        for copy in smalls:
            copy.wait()
        own_copy.wait()
        for q in range(1, verts):
            first_copy(q).wait_recv()

    def remote(src, dst, send_sem, recv_sem, device):
        return pltpu.make_async_remote_copy(
            src_ref=src, dst_ref=dst, send_sem=send_sem, recv_sem=recv_sem, device_id=device, device_id_type=MESH
        )

    beside = (base + (slot + 1) % group, core)
    onward = (jnp.minimum(me + group, owners - 1), core)
    others = (group - 1) * snaps

    def a_mark(w, d):
        return 2 * w + (1 if d == group - 1 else 0) if w < early else w + early

    def a_copy(l, w, d):
        owner = partner(d)
        return remote(
            sent_graph.at[l, w, :, strip(owner)], window.at[l, w, pl.ds(held + slot * snaps, snaps)],
            a_send, a_recv.at[a_mark(w, d)], (base + owner, core),
        )

    def a_some(l, w, count, d):
        part = window.at[l, w, pl.ds(0, count * snaps)]
        return remote(part, part, a_send, a_recv.at[a_mark(w, d)], beside)

    def z_copy(l, w, start, count):
        return remote(
            window.at[l, w, pl.ds(held + start, count)], window.at[l, w, pl.ds(start, count)],
            z_send, z_recv.at[l, w], onward,
        )

    def z_all(l, w):
        return z_copy(l, w, unused, held - unused)

    def z_half(l, w, half):
        span = pl.ds(half * (rows // 2), rows // 2)
        arrived = z_recv.at[l, w] if half == 0 else z_late.at[l]
        return remote(
            window.at[l, w, pl.ds(held + unused, held - unused), span],
            window.at[l, w, pl.ds(unused, held - unused), span], z_send, arrived, onward,
        )

    def z_origin(l, w, origin):
        if unused == 0:
            z_copy(l, w, origin * snaps, snaps).start()
            return

        @pl.when(origin == 0)
        def _():
            z_copy(l, w, skip, snaps - skip).start()

        @pl.when(origin > 0)
        def _():
            z_copy(l, w, origin * snaps, snaps).start()

    def b_mark(l, w):
        return l * apart + w if l < layers - 1 else (layers - 1) * apart

    def target(l, w, top, size):
        r = far_tiles[w]
        place = out.at[:, r] if l == layers - 1 else full[l + 1].at[:, first_tile + r]
        return place.at[:, pl.ds(pl.multiple_of(slot * rows + top, STRIP), size)]

    def b_copy(l, w, d, top, size):
        home = partner(d)
        return remote(
            sent_time.at[l, w, pl.ds(home * snaps, snaps), pl.ds(top, size)], target(l, w, top, size),
            b_send, b_recv.at[b_mark(l, w)], (base + home, core),
        )

    def cross_copy(l, d, q, top, size):
        home = partner(d)
        return remote(
            sent_time.at[l, apart - 1, pl.ds(home * snaps, snaps), pl.ds(top, size)], target(l, apart - 1, top, size),
            cross_send.at[l, q - 1], cross_recv.at[l, q - 1], (base + home, (core + q) % verts),
        )

    def cross_all(l, q):
        part = full[l + 1].at[:, first_tile + tiles - 1]
        return remote(part, part, cross_send.at[l, q - 1], cross_recv.at[l, q - 1], (me, (core + q) % verts))

    def b_all(l, w):
        part = sent_time.at[l, w, pl.ds(0, others)] if l < layers - 1 else sent_time.at[l, :, pl.ds(0, others)]
        return remote(part, part, b_send, b_recv.at[b_mark(l, w)], beside)

    def out_copy(w, top, size):
        own = sent_time.at[layers - 1, w, pl.ds(slot * snaps, snaps), pl.ds(top, size)]
        return pltpu.make_async_copy(own, target(layers - 1, w, top, size), out_sem)

    def v_copy(l, part, q):
        return remote(part, part, v_send.at[l, q - 1], v_recv.at[l, q - 1], (me, (core + q) % verts))

    def v_all(l, q):
        return v_copy(l, full[l + 1].at[:, pl.ds(first_tile, tiles - 1)], q)

    def v_start(l, r):
        for q in range(1, verts):
            v_copy(l, full[l + 1].at[:, first_tile + r], q).start()

    def nz_copy(l, n, first):
        return remote(
            near.at[l, n, pl.ds(2 * snaps + first, snaps - first)], near.at[l, n, pl.ds(first, snaps - first)],
            nz_send, nz_recv.at[l, n], onward,
        )

    def nz_do(act):
        if skip == 0:
            act(0)
            return

        @pl.when(slot == 0)
        def _():
            act(skip)

        @pl.when(slot > 0)
        def _():
            act(0)

    def ny_copy(l, n):
        return remote(
            near.at[l, n, pl.ds(2 * snaps * (1 - slot_y), snaps)], near.at[l, n, pl.ds(snaps, snaps)],
            ny_send, ny_recv.at[l, n], (base + (slot + 2) % group, core),
        )

    def nx_copy(l, n):
        return remote(
            part_out.at[l, n], part_in.at[l, n], nx_send, nx_recv.at[l, n], (base + slot + 1 - 2 * slot_x, core)
        )

    def lag_sum(l, i, sources):
        total = None
        for apart_by, values in sources:
            for j in range(snaps):
                lag = apart_by * snaps + i - j
                if 0 <= lag < lags:
                    term = lag_mix[l, lag:lag + 1] * values[j]
                    total = term if total is None else total + term
        return total

    def near_load(l, n, first, span):
        return [near[l, n, first + j, span].astype(jnp.float32) for j in range(snaps)]

    def near_y(l, n):
        @pl.when(slot_y == 1)
        def _():
            @pl.when(plane > 0)
            def _():
                nz_do(lambda first: nz_copy(l, n, first).wait_recv())

            ny_copy(l, n).start()

        @pl.when(slot_y == 0)
        def _():
            ny_copy(l, n).start()

    def near_x(l, n):
        @pl.when((slot_y == 0) & (plane > 0))
        def _():
            nz_do(lambda first: nz_copy(l, n, first).wait_recv())

        ny_copy(l, n).wait_recv()
        for top in range(0, tile, STRIP):
            span = slice(top, top + STRIP)
            newer = near_load(l, n, snaps * (2 - slot_x), span)
            older = near_load(l, n, snaps * (1 - slot_x), span)
            for i in range(snaps):
                part_out[l, n, i, span] = lag_sum(l, i, [(1, newer), (3, older)]).astype(jnp.bfloat16)
        nx_copy(l, n).start()

    def near_time(l, n):
        r = near_tiles[n]
        nx_copy(l, n).wait_recv()
        spots, mixes, states = [], [], []
        for top in range(0, tile, STRIP):
            span = slice(top, top + STRIP)
            seen = [near_load(l, n, snaps * p, span) for p in range(3)]
            for i in range(snaps):
                mixed = lag_sum(l, i, [(0, seen[2]), (2, seen[1]), (4, seen[0])])
                mixes.append(mixed + part_in[l, n, i, span].astype(jnp.float32))
                states.append(seen[2][i])
                spots.append((i, span))
        branch = mlp(normalise(jnp.concatenate(mixes, axis=0), time_gain[l:l + 1]), time_up[l], time_down[l])
        result = (jnp.concatenate(states, axis=0) + branch).astype(jnp.bfloat16)
        for k, (i, span) in enumerate(spots):
            piece = result[k * STRIP:(k + 1) * STRIP]
            if l == layers - 1:
                near_done[n, i, span] = piece
            else:
                full[l + 1][i, first_tile + r, span] = piece
        if l == layers - 1:
            near_out(n).start()
        else:
            v_start(l, r)

    def near_out(n):
        return pltpu.make_async_copy(near_done.at[n], out.at[:, near_tiles[n]], near_sem)

    def graph_step(l, r):
        if l == 0 and r > 0:
            convert(r)
        sums = []
        for t in range(snaps):
            picked = jnp.concatenate([full[l][t, cols[t, r, k]] for k in range(picks)], axis=0)
            sums.append(jnp.dot(blocks[t, r], picked, preferred_element_type=jnp.float32))
        summed = jnp.concatenate(sums, axis=0)
        branch = mlp(normalise(summed, graph_gain[l:l + 1]), graph_up[l], graph_down[l])
        state = full[l][:, first_tile + r].astype(jnp.float32)
        result = (state + branch.reshape(snaps, tile, width)).astype(jnp.bfloat16)
        if r in near_tiles:
            n = near_tiles.index(r)
            near[l, n, 2 * snaps:3 * snaps] = result

            @pl.when(plane < groups - 1)
            def _():
                nz_do(lambda first: nz_copy(l, n, first).start())

            return
        w = far_tiles.index(r)
        sent_graph[l, w] = result
        for d in range(1, group) if w < early else reversed(range(1, group)):
            a_copy(l, w, d).start()
        window[l, w, pl.ds(held + slot * snaps, snaps)] = sent_graph[l, w, :, strip(slot)]

        if w < sooner:

            @pl.when(plane < groups - 1)
            def _():
                z_origin(l, w, slot)

    def forward(l, w, parts):
        a_some(l, w, len(parts), parts[-1]).wait_recv()

        @pl.when(plane < groups - 1)
        def _():
            if w < sooner:
                for d in parts:
                    z_origin(l, w, partner(d, True))
            elif w in halved:
                z_half(l, w, 0).start()
                z_half(l, w, 1).start()
            else:
                z_all(l, w).start()

    def forward_most(l, w):
        forward(l, w, range(1, group - 1))

    def forward_last(l, w):
        forward(l, w, [group - 1])

    def forward_all(l, w):
        forward(l, w, range(1, group))

    def time_step(l, w):
        @pl.when(plane > 0)
        def _():
            z_all(l, w).wait_recv()

        time_rows(l, w, 0, rows)

    def time_half(l, w, half):
        @pl.when(plane > 0)
        def _():
            z_half(l, w, half).wait_recv()

        time_rows(l, w, half * (rows // 2), rows // 2)

    def time_rows(l, w, start, size):
        spots, mixes, states = [], [], []
        for top in range(start, start + size, STRIP):
            span = slice(top, top + STRIP)
            seen = {i: window[l, w, i, span].astype(jnp.float32) for i in range(unused, 2 * held)}
            for i in range(held):
                mixed = lag_mix[l, 0:1] * seen[held + i]
                for m in range(1, lags):
                    mixed = mixed + lag_mix[l, m:m + 1] * seen[held + i - m]
                spots.append((i, span))
                mixes.append(mixed)
                states.append(seen[held + i])
        branch = mlp(normalise(jnp.concatenate(mixes, axis=0), time_gain[l:l + 1]), time_up[l], time_down[l])
        result = (jnp.concatenate(states, axis=0) + branch).astype(jnp.bfloat16)
        for n, (i, span) in enumerate(spots):
            sent_time[l, w, i, span] = result[n * STRIP:(n + 1) * STRIP]
        crossing = l < layers - 1 and w == apart - 1
        for d in reversed(range(1, group)):
            b_copy(l, w, d, start, size).start()
            if crossing:
                for q in range(1, verts):
                    cross_copy(l, d, q, start, size).start()
        if crossing:
            for q in range(1, verts):
                cross_copy(l, 0, q, start, size).start()
        if l == layers - 1:
            out_copy(w, start, size).start()
        else:
            own = sent_time[l, w, pl.ds(slot * snaps, snaps), start:start + size]
            place = pl.ds(pl.multiple_of(slot * rows + start, STRIP), size)
            full[l + 1][:, first_tile + far_tiles[w], place] = own

    def collect(l, w):
        b_all(l, w).wait_recv()
        if w < apart - 1:
            v_start(l, far_tiles[w])

    def run(kind, step, l, n):
        with jax.named_scope(f"{kind}{l}_{n}"):
            step(l, n)

    for l in range(layers):
        if l == 0:
            for i in range(2):
                far_copies[i].wait()
        ready = {}
        for w in range(early):
            ready.setdefault(min(far_tiles[w] + BEHIND + 1, tiles - 1), []).append(("fl", forward_last, w))
            ready.setdefault(min(far_tiles[w] + BEHIND, tiles - 1), []).append(("fm", forward_most, w))
        for r in range(tiles):
            run("g", graph_step, l, r)
            if r == tiles - SIDEWAYS:
                for n in range(count):
                    run("y", near_y, l, n)
            for kind, step, w in sorted(ready.get(r, []), key=lambda item: (item[2], item[0] == "fl")):
                run(kind, step, l, w)
        if l == 0:
            for i in range(2, 4):
                far_copies[i].wait()
        passed = early
        for w in range(apart):
            while passed < min(w + BEHIND, apart):
                run("f", forward_all, l, passed)
                passed += 1
            if w in halved:
                for half in range(2):
                    with jax.named_scope(f"t{l}_{w}_{half}"):
                        time_half(l, w, half)
            else:
                run("t", time_step, l, w)
            for n in range(count):
                if w == min(CROSSING + l, apart - 1):

                    @pl.when(plane > l)
                    def _():
                        run("x", near_x, l, n)

                if w == min(FIRST_CROSSING, apart - 1):

                    @pl.when(plane <= l)
                    def _():
                        run("x", near_x, l, n)

        for n in range(count):
            run("n", near_time, l, n)
        if l < layers - 1:
            for w in range(apart):
                run("c", collect, l, w)
            with jax.named_scope(f"v{l}"):
                for q in range(1, verts):
                    cross_all(l, q).wait_recv()
                    v_all(l, q).wait_recv()
        else:
            with jax.named_scope(f"c{l}"):
                b_all(l, 0).wait_recv()

    with jax.named_scope("drain"):
        for q in range(1, verts):
            first_copy(q).wait_send()
        part = out.at[:, pl.ds(0, apart), pl.ds(0, rows)]
        pltpu.make_async_copy(part, part, out_sem).wait()
        part = window.at[:, :, pl.ds(0, others)]
        remote(part, part, a_send, a_recv.at[0], beside).wait_send()
        part = sent_time.at[:, :, pl.ds(0, others)]
        remote(part, part, b_send, b_recv.at[0], beside).wait_send()
        for l in range(layers - 1):
            for q in range(1, verts):
                v_all(l, q).wait_send()
                cross_all(l, q).wait_send()

        @pl.when(plane < groups - 1)
        def _():
            part = window.at[:, :, pl.ds(unused, held - unused)]
            remote(part, part, z_send, z_recv.at[0, 0], onward).wait_send()

        if count > 0:
            part = out.at[:, pl.ds(0, count)]
            pltpu.make_async_copy(part, part, near_sem).wait()
            part = near.at[:, :, pl.ds(0, snaps)]
            remote(part, part, ny_send, ny_recv.at[0, 0], beside).wait_send()
            remote(part_out, part_out, nx_send, nx_recv.at[0, 0], beside).wait_send()

            @pl.when(plane < groups - 1)
            def _():
                def take(first):
                    part = near.at[:, :, pl.ds(first, snaps - first)]
                    remote(part, part, nz_send, nz_recv.at[0, 0], onward).wait_send()

                nz_do(take)


def near_list(group, tiles):
    return [1] if group == 4 and tiles > 4 else []


def on_device(owners, verts, features, tile_cols, tile_weights, graph_gain, graph_up, graph_down, lag_mix, time_gain, time_up, time_down):
    snaps, vert_dev, width = features.shape
    _, tiles, picks, tile, _ = tile_weights.shape
    layers, lags = lag_mix.shape[0], lag_mix.shape[1]
    group = -(-(lags - 1) // snaps)
    while owners % group or tile % (group * STRIP):
        group += 1
    rows = tile // group
    held = group * snaps
    near_count = len(near_list(group, tiles))
    apart, count = tiles - near_count, max(near_count, 1)
    bf16 = jnp.bfloat16
    dma = pltpu.SemaphoreType.DMA
    result = pl.pallas_call(
        functools.partial(kernel, owners, verts, group),
        out_shape=jax.ShapeDtypeStruct((snaps, tiles, tile, width), bf16),
        in_specs=[pl.BlockSpec(memory_space=pltpu.HBM)] * 10,
        out_specs=pl.BlockSpec(memory_space=pl.ANY),
        scratch_shapes=[pltpu.VMEM((snaps, verts * tiles, tile, width), bf16)] * layers + [
            pltpu.VMEM((snaps, tiles, picks, tile, tile), jnp.int32),
            pltpu.VMEM((snaps, tiles, tile, picks * tile), bf16),
            pltpu.VMEM((layers, apart, snaps, tile, width), bf16),
            pltpu.VMEM((layers, apart, 2 * held, rows, width), bf16),
            pltpu.VMEM((layers, apart, held, rows, width), bf16),
            pltpu.VMEM((layers, count, 3 * snaps, tile, width), bf16),
            pltpu.VMEM((layers, count, snaps, tile, width), bf16),
            pltpu.VMEM((layers, count, snaps, tile, width), bf16),
            pltpu.VMEM((count, snaps, tile, width), bf16),
            pltpu.VMEM(graph_up.shape, bf16),
            pltpu.VMEM(graph_down.shape, bf16),
            pltpu.VMEM(time_up.shape, bf16),
            pltpu.VMEM(time_down.shape, bf16),
            dma,
            dma((4,)),
            dma((tiles // 2 + 1,)),
            dma((verts - 1,)),
            dma((verts - 1,)),
            dma,
            dma((apart + min(EARLY, apart),)),
            dma((layers - 1, verts - 1)),
            dma((layers - 1, verts - 1)),
            dma,
            dma((layers, apart)),
            dma((layers,)),
            dma,
            dma(((layers - 1) * apart + 1,)),
            dma((layers - 1, verts - 1)),
            dma((layers - 1, verts - 1)),
            dma,
        ] + [dma, dma((layers, count))] * 3 + [
            dma,
            pltpu.SMEM(tile_cols.shape, jnp.int32),
            pltpu.VMEM(graph_gain.shape, jnp.float32),
            pltpu.VMEM(lag_mix.shape, jnp.float32),
            pltpu.VMEM(time_gain.shape, jnp.float32),
            dma((4,)),
        ],
        compiler_params=pltpu.CompilerParams(
            collective_id=0, has_side_effects=True, vmem_limit_bytes=36 * 1024 * 1024
        ),
    )(
        *[pltpu.with_memory_space_constraint(array, pltpu.HBM) for array in (
            features.reshape(snaps, tiles, tile, width), tile_cols, tile_weights,
            graph_gain, lag_mix, time_gain, graph_up, graph_down, time_up, time_down,
        )]
    )
    return result.reshape(features.shape)


def solution(mesh):
    return jax.shard_map(
        functools.partial(on_device, mesh.shape["snap"], mesh.shape["vert"]),
        mesh=mesh,
        in_specs=(
            P("snap", "vert", None),
            P("snap", "vert", None),
            P("snap", "vert", None, None, None),
        ) + (P(),) * 7,
        out_specs=P("snap", "vert", None),
        check_vma=False,
    )
```

```python
import functools

import jax
import jax.numpy as jnp
from jax import lax
from jax.experimental import pallas as pl
from jax.experimental.pallas import tpu as pltpu
from jax.sharding import PartitionSpec as P

eps = 1e-06
MESH = pl.DeviceIdType.MESH
STRIP = 16
GELU_A = 0.7978845608028654
GELU_B = GELU_A * 0.044715
EARLY = 3
SOONER = 8
CROSSING = 2
FIRST_CROSSING = 4
SIDEWAYS = 1
BEHIND = 4


def normalise(rows, gain_row):
    scale = lax.rsqrt(jnp.mean(rows * rows, axis=-1, keepdims=True) + eps)
    return (rows * scale * gain_row).astype(jnp.bfloat16)


def mlp(normed, up_weight, down_weight):
    hidden = jnp.dot(normed, up_weight, preferred_element_type=jnp.float32)
    hidden = hidden.astype(jnp.bfloat16)
    inner = hidden * (GELU_A + GELU_B * (hidden * hidden))
    half = hidden * 0.5
    hidden = half + half * jnp.tanh(inner)
    return jnp.dot(hidden, down_weight, preferred_element_type=jnp.float32)


def kernel(
    owners, verts, group,
    feats, cols_far, weights, graph_gain_far, lag_mix_far, time_gain_far, graph_up_far, graph_down_far, time_up_far, time_down_far,
    out, *scratch,
):
    layers = lag_mix_far.shape[0]
    full = scratch[:layers]
    (
        raw, blocks, sent_graph, window, sent_time, near, part_out, part_in, near_done,
        graph_up, graph_down, time_up, time_down, own_sem, far_sem, raw_sem, first_send, first_recv,
        a_send, a_recv, cross_send, cross_recv, z_send, z_recv, z_late, b_send, b_recv, v_send, v_recv, out_sem,
        nz_send, nz_recv, ny_send, ny_recv, nx_send, nx_recv, near_sem,
        cols, graph_gain, lag_mix, time_gain, small_sem,
    ) = scratch[layers:]
    snaps, tiles, tile, width = feats.shape
    picks = weights.shape[2]
    lags = lag_mix_far.shape[1]
    rows = window.shape[3]
    held = group * snaps
    unused = held - (lags - 1)
    groups = owners // group
    near_tiles = near_list(group, tiles)
    far_tiles = [r for r in range(tiles) if r not in near_tiles]
    apart, count = len(far_tiles), len(near_tiles)
    early = min(EARLY, apart)
    halved = [apart - 1] if rows % (2 * STRIP) == 0 and apart > early else []
    sooner = min(SOONER, apart - len(halved))
    skip = min(unused, snaps - 1)

    me = lax.axis_index("snap")
    core = lax.axis_index("vert")
    slot = me % group
    plane = me // group
    base = me - slot
    first_tile = core * tiles
    slot_x, slot_y = slot % 2, slot // 2

    def partner(d, back=False):
        if group == 4:
            return (slot + d) % 2 + 2 * ((slot // 2 + d // 2) % 2)
        return (slot + (group - d if back else d)) % group

    def strip(owner):
        return pl.ds(pl.multiple_of(owner * rows, rows), rows)

    far_copies = [
        pltpu.make_async_copy(far, near, far_sem.at[i])
        for i, (far, near) in enumerate([
            (graph_up_far, graph_up), (graph_down_far, graph_down), (time_up_far, time_up), (time_down_far, time_down)
        ])
    ]
    loads = [(r, 1) for r in range(min(2, tiles))]
    while sum(loads[-1]) < tiles:
        loads.append((sum(loads[-1]), min(2, tiles - sum(loads[-1]))))

    def raw_copy(i):
        span = pl.ds(*loads[i])
        return pltpu.make_async_copy(weights.at[:, span], raw.at[:, span], raw_sem.at[i])

    smalls = [
        pltpu.make_async_copy(src, dst, small_sem.at[i])
        for i, (src, dst) in enumerate(
            [(cols_far, cols), (graph_gain_far, graph_gain), (lag_mix_far, lag_mix), (time_gain_far, time_gain)]
        )
    ]
    own_copy = pltpu.make_async_copy(feats, full[0].at[:, pl.ds(first_tile, tiles)], own_sem)
    barrier = pltpu.get_barrier_semaphore()
    for q in range(verts):
        for d in range(group):
            if q + d > 0:
                pl.semaphore_signal(
                    barrier, inc=1, device_id=(base + partner(d), (core + q) % verts), device_id_type=MESH
                )

    @pl.when(plane > 0)
    def _():
        pl.semaphore_signal(barrier, inc=1, device_id=(me - group, core), device_id_type=MESH)

    @pl.when(plane < groups - 1)
    def _():
        pl.semaphore_signal(barrier, inc=1, device_id=(me + group, core), device_id_type=MESH)

    own_copy.start()
    for copy in smalls:
        copy.start()
    raw_copy(0).start()

    @pl.when(plane == 0)
    def _():
        for l in range(layers):
            for w in range(apart):
                window[l, w, 0:held] = jnp.zeros((held, rows, width), jnp.bfloat16)
            for n in range(count):
                near[l, n, 0:snaps] = jnp.zeros((snaps, tile, width), jnp.bfloat16)

    ahead = jnp.where(plane < groups - 1, 1, 0)
    behind = jnp.where(plane > 0, 1, 0)
    with jax.named_scope("barrier"):
        pl.semaphore_wait(barrier, group * verts - 1 + ahead + behind)

    def first_copy(q):
        return pltpu.make_async_remote_copy(
            src_ref=feats,
            dst_ref=full[0].at[:, pl.ds(first_tile, tiles)],
            send_sem=first_send.at[q - 1],
            recv_sem=first_recv.at[q - 1],
            device_id=(me, (core + q) % verts),
            device_id_type=MESH,
        )

    for q in range(1, verts):
        first_copy(q).start()
    for i in range(2):
        far_copies[i].start()
    for i in range(1, len(loads)):
        raw_copy(i).start()
    for i in range(2, 4):
        far_copies[i].start()

    def convert(r):
        for i, (first, _) in enumerate(loads):
            if first == r:
                raw_copy(i).wait()
        for t in range(snaps):
            blocks[t, r] = jnp.concatenate(
                [raw[t, r, k].astype(jnp.float32).astype(jnp.bfloat16) for k in range(picks)], axis=1
            )

    with jax.named_scope("k0"):
        convert(0)

    with jax.named_scope("first"):
        for copy in smalls:
            copy.wait()
        own_copy.wait()
        for q in range(1, verts):
            first_copy(q).wait_recv()

    def remote(src, dst, send_sem, recv_sem, device):
        return pltpu.make_async_remote_copy(
            src_ref=src, dst_ref=dst, send_sem=send_sem, recv_sem=recv_sem, device_id=device, device_id_type=MESH
        )

    beside = (base + (slot + 1) % group, core)
    onward = (jnp.minimum(me + group, owners - 1), core)
    others = (group - 1) * snaps

    def a_mark(w, d):
        return 2 * w + (1 if d == group - 1 else 0) if w < early else w + early

    def a_copy(l, w, d):
        owner = partner(d)
        return remote(
            sent_graph.at[l, w, :, strip(owner)], window.at[l, w, pl.ds(held + slot * snaps, snaps)],
            a_send, a_recv.at[a_mark(w, d)], (base + owner, core),
        )

    def a_some(l, w, count, d):
        part = window.at[l, w, pl.ds(0, count * snaps)]
        return remote(part, part, a_send, a_recv.at[a_mark(w, d)], beside)

    def z_copy(l, w, start, count):
        return remote(
            window.at[l, w, pl.ds(held + start, count)], window.at[l, w, pl.ds(start, count)],
            z_send, z_recv.at[l, w], onward,
        )

    def z_all(l, w):
        return z_copy(l, w, unused, held - unused)

    def z_half(l, w, half):
        span = pl.ds(half * (rows // 2), rows // 2)
        arrived = z_recv.at[l, w] if half == 0 else z_late.at[l]
        return remote(
            window.at[l, w, pl.ds(held + unused, held - unused), span],
            window.at[l, w, pl.ds(unused, held - unused), span], z_send, arrived, onward,
        )

    def z_origin(l, w, origin):
        if unused == 0:
            z_copy(l, w, origin * snaps, snaps).start()
            return

        @pl.when(origin == 0)
        def _():
            z_copy(l, w, skip, snaps - skip).start()

        @pl.when(origin > 0)
        def _():
            z_copy(l, w, origin * snaps, snaps).start()

    def b_mark(l, w):
        return l * apart + w if l < layers - 1 else (layers - 1) * apart

    def target(l, w, top, size):
        r = far_tiles[w]
        place = out.at[:, r] if l == layers - 1 else full[l + 1].at[:, first_tile + r]
        return place.at[:, pl.ds(pl.multiple_of(slot * rows + top, STRIP), size)]

    def b_copy(l, w, d, top, size):
        home = partner(d)
        return remote(
            sent_time.at[l, w, pl.ds(home * snaps, snaps), pl.ds(top, size)], target(l, w, top, size),
            b_send, b_recv.at[b_mark(l, w)], (base + home, core),
        )

    def cross_copy(l, d, q, top, size):
        home = partner(d)
        return remote(
            sent_time.at[l, apart - 1, pl.ds(home * snaps, snaps), pl.ds(top, size)], target(l, apart - 1, top, size),
            cross_send.at[l, q - 1], cross_recv.at[l, q - 1], (base + home, (core + q) % verts),
        )

    def cross_all(l, q):
        part = full[l + 1].at[:, first_tile + tiles - 1]
        return remote(part, part, cross_send.at[l, q - 1], cross_recv.at[l, q - 1], (me, (core + q) % verts))

    def b_all(l, w):
        part = sent_time.at[l, w, pl.ds(0, others)] if l < layers - 1 else sent_time.at[l, :, pl.ds(0, others)]
        return remote(part, part, b_send, b_recv.at[b_mark(l, w)], beside)

    def out_copy(w, top, size):
        own = sent_time.at[layers - 1, w, pl.ds(slot * snaps, snaps), pl.ds(top, size)]
        return pltpu.make_async_copy(own, target(layers - 1, w, top, size), out_sem)

    def v_copy(l, part, q):
        return remote(part, part, v_send.at[l, q - 1], v_recv.at[l, q - 1], (me, (core + q) % verts))

    def v_all(l, q):
        return v_copy(l, full[l + 1].at[:, pl.ds(first_tile, tiles - 1)], q)

    def v_start(l, r):
        for q in range(1, verts):
            v_copy(l, full[l + 1].at[:, first_tile + r], q).start()

    def nz_copy(l, n, first):
        return remote(
            near.at[l, n, pl.ds(2 * snaps + first, snaps - first)], near.at[l, n, pl.ds(first, snaps - first)],
            nz_send, nz_recv.at[l, n], onward,
        )

    def nz_do(act):
        if skip == 0:
            act(0)
            return

        @pl.when(slot == 0)
        def _():
            act(skip)

        @pl.when(slot > 0)
        def _():
            act(0)

    def ny_copy(l, n):
        return remote(
            near.at[l, n, pl.ds(2 * snaps * (1 - slot_y), snaps)], near.at[l, n, pl.ds(snaps, snaps)],
            ny_send, ny_recv.at[l, n], (base + (slot + 2) % group, core),
        )

    def nx_copy(l, n):
        return remote(
            part_out.at[l, n], part_in.at[l, n], nx_send, nx_recv.at[l, n], (base + slot + 1 - 2 * slot_x, core)
        )

    def lag_sum(l, i, sources):
        total = None
        for apart_by, values in sources:
            for j in range(snaps):
                lag = apart_by * snaps + i - j
                if 0 <= lag < lags:
                    term = lag_mix[l, lag:lag + 1] * values[j]
                    total = term if total is None else total + term
        return total

    def near_load(l, n, first, span):
        return [near[l, n, first + j, span].astype(jnp.float32) for j in range(snaps)]

    def near_y(l, n):
        @pl.when(slot_y == 1)
        def _():
            @pl.when(plane > 0)
            def _():
                nz_do(lambda first: nz_copy(l, n, first).wait_recv())

            ny_copy(l, n).start()

        @pl.when(slot_y == 0)
        def _():
            ny_copy(l, n).start()

    def near_x(l, n):
        @pl.when((slot_y == 0) & (plane > 0))
        def _():
            nz_do(lambda first: nz_copy(l, n, first).wait_recv())

        ny_copy(l, n).wait_recv()
        for top in range(0, tile, STRIP):
            span = slice(top, top + STRIP)
            newer = near_load(l, n, snaps * (2 - slot_x), span)
            older = near_load(l, n, snaps * (1 - slot_x), span)
            for i in range(snaps):
                part_out[l, n, i, span] = lag_sum(l, i, [(1, newer), (3, older)]).astype(jnp.bfloat16)
        nx_copy(l, n).start()

    def near_time(l, n):
        r = near_tiles[n]
        nx_copy(l, n).wait_recv()
        spots, mixes, states = [], [], []
        for top in range(0, tile, STRIP):
            span = slice(top, top + STRIP)
            seen = [near_load(l, n, snaps * p, span) for p in range(3)]
            for i in range(snaps):
                mixed = lag_sum(l, i, [(0, seen[2]), (2, seen[1]), (4, seen[0])])
                mixes.append(mixed + part_in[l, n, i, span].astype(jnp.float32))
                states.append(seen[2][i])
                spots.append((i, span))
        branch = mlp(normalise(jnp.concatenate(mixes, axis=0), time_gain[l:l + 1]), time_up[l], time_down[l])
        result = (jnp.concatenate(states, axis=0) + branch).astype(jnp.bfloat16)
        for k, (i, span) in enumerate(spots):
            piece = result[k * STRIP:(k + 1) * STRIP]
            if l == layers - 1:
                near_done[n, i, span] = piece
            else:
                full[l + 1][i, first_tile + r, span] = piece
        if l == layers - 1:
            near_out(n).start()
        else:
            v_start(l, r)

    def near_out(n):
        return pltpu.make_async_copy(near_done.at[n], out.at[:, near_tiles[n]], near_sem)

    def graph_step(l, r):
        if l == 0 and r > 0:
            convert(r)
        sums = []
        for t in range(snaps):
            picked = jnp.concatenate([full[l][t, cols[t, r, k]] for k in range(picks)], axis=0)
            sums.append(jnp.dot(blocks[t, r], picked, preferred_element_type=jnp.float32))
        summed = jnp.concatenate(sums, axis=0)
        branch = mlp(normalise(summed, graph_gain[l:l + 1]), graph_up[l], graph_down[l])
        state = full[l][:, first_tile + r].astype(jnp.float32)
        result = (state + branch.reshape(snaps, tile, width)).astype(jnp.bfloat16)
        if r in near_tiles:
            n = near_tiles.index(r)
            near[l, n, 2 * snaps:3 * snaps] = result

            @pl.when(plane < groups - 1)
            def _():
                nz_do(lambda first: nz_copy(l, n, first).start())

            return
        w = far_tiles.index(r)
        sent_graph[l, w] = result
        for d in range(1, group) if w < early else reversed(range(1, group)):
            a_copy(l, w, d).start()
        window[l, w, pl.ds(held + slot * snaps, snaps)] = sent_graph[l, w, :, strip(slot)]

        if w < sooner:

            @pl.when(plane < groups - 1)
            def _():
                z_origin(l, w, slot)

    def forward(l, w, parts):
        a_some(l, w, len(parts), parts[-1]).wait_recv()

        @pl.when(plane < groups - 1)
        def _():
            if w < sooner:
                for d in parts:
                    z_origin(l, w, partner(d, True))
            elif w in halved:
                z_half(l, w, 0).start()
                z_half(l, w, 1).start()
            else:
                z_all(l, w).start()

    def forward_most(l, w):
        forward(l, w, range(1, group - 1))

    def forward_last(l, w):
        forward(l, w, [group - 1])

    def forward_all(l, w):
        forward(l, w, range(1, group))

    def time_step(l, w):
        @pl.when(plane > 0)
        def _():
            z_all(l, w).wait_recv()

        time_rows(l, w, 0, rows)

    def time_half(l, w, half):
        @pl.when(plane > 0)
        def _():
            z_half(l, w, half).wait_recv()

        time_rows(l, w, half * (rows // 2), rows // 2)

    def time_rows(l, w, start, size):
        spots, mixes, states = [], [], []
        for top in range(start, start + size, STRIP):
            span = slice(top, top + STRIP)
            seen = {i: window[l, w, i, span].astype(jnp.float32) for i in range(unused, 2 * held)}
            for i in range(held):
                mixed = lag_mix[l, 0:1] * seen[held + i]
                for m in range(1, lags):
                    mixed = mixed + lag_mix[l, m:m + 1] * seen[held + i - m]
                spots.append((i, span))
                mixes.append(mixed)
                states.append(seen[held + i])
        branch = mlp(normalise(jnp.concatenate(mixes, axis=0), time_gain[l:l + 1]), time_up[l], time_down[l])
        result = (jnp.concatenate(states, axis=0) + branch).astype(jnp.bfloat16)
        for n, (i, span) in enumerate(spots):
            sent_time[l, w, i, span] = result[n * STRIP:(n + 1) * STRIP]
        crossing = l < layers - 1 and w == apart - 1
        for d in reversed(range(1, group)):
            b_copy(l, w, d, start, size).start()
            if crossing:
                for q in range(1, verts):
                    cross_copy(l, d, q, start, size).start()
        if crossing:
            for q in range(1, verts):
                cross_copy(l, 0, q, start, size).start()
        if l == layers - 1:
            out_copy(w, start, size).start()
        else:
            own = sent_time[l, w, pl.ds(slot * snaps, snaps), start:start + size]
            place = pl.ds(pl.multiple_of(slot * rows + start, STRIP), size)
            full[l + 1][:, first_tile + far_tiles[w], place] = own

    def collect(l, w):
        b_all(l, w).wait_recv()
        if w < apart - 1:
            v_start(l, far_tiles[w])

    def run(kind, step, l, n):
        with jax.named_scope(f"{kind}{l}_{n}"):
            step(l, n)

    for l in range(layers):
        if l == 0:
            for i in range(2):
                far_copies[i].wait()
        ready = {}
        for w in range(early):
            ready.setdefault(min(far_tiles[w] + BEHIND + 1, tiles - 1), []).append(("fl", forward_last, w))
            ready.setdefault(min(far_tiles[w] + BEHIND, tiles - 1), []).append(("fm", forward_most, w))
        for r in range(tiles):
            run("g", graph_step, l, r)
            if r == tiles - SIDEWAYS:
                for n in range(count):
                    run("y", near_y, l, n)
            for kind, step, w in sorted(ready.get(r, []), key=lambda item: (item[2], item[0] == "fl")):
                run(kind, step, l, w)
        if l == 0:
            for i in range(2, 4):
                far_copies[i].wait()
        passed = early
        for w in range(apart):
            while passed < min(w + BEHIND, apart):
                run("f", forward_all, l, passed)
                passed += 1
            if w in halved:
                for half in range(2):
                    with jax.named_scope(f"t{l}_{w}_{half}"):
                        time_half(l, w, half)
            else:
                run("t", time_step, l, w)
            for n in range(count):
                if w == min(CROSSING + l, apart - 1):

                    @pl.when(plane > l)
                    def _():
                        run("x", near_x, l, n)

                if w == min(FIRST_CROSSING, apart - 1):

                    @pl.when(plane <= l)
                    def _():
                        run("x", near_x, l, n)

        for n in range(count):
            run("n", near_time, l, n)
        if l < layers - 1:
            for w in range(apart):
                run("c", collect, l, w)
            with jax.named_scope(f"v{l}"):
                for q in range(1, verts):
                    cross_all(l, q).wait_recv()
                    v_all(l, q).wait_recv()
        else:
            with jax.named_scope(f"c{l}"):
                b_all(l, 0).wait_recv()

    with jax.named_scope("drain"):
        for q in range(1, verts):
            first_copy(q).wait_send()
        part = out.at[:, pl.ds(0, apart), pl.ds(0, rows)]
        pltpu.make_async_copy(part, part, out_sem).wait()
        part = window.at[:, :, pl.ds(0, others)]
        remote(part, part, a_send, a_recv.at[0], beside).wait_send()
        part = sent_time.at[:, :, pl.ds(0, others)]
        remote(part, part, b_send, b_recv.at[0], beside).wait_send()
        for l in range(layers - 1):
            for q in range(1, verts):
                v_all(l, q).wait_send()
                cross_all(l, q).wait_send()

        @pl.when(plane < groups - 1)
        def _():
            part = window.at[:, :, pl.ds(unused, held - unused)]
            remote(part, part, z_send, z_recv.at[0, 0], onward).wait_send()

        if count > 0:
            part = out.at[:, pl.ds(0, count)]
            pltpu.make_async_copy(part, part, near_sem).wait()
            part = near.at[:, :, pl.ds(0, snaps)]
            remote(part, part, ny_send, ny_recv.at[0, 0], beside).wait_send()
            remote(part_out, part_out, nx_send, nx_recv.at[0, 0], beside).wait_send()

            @pl.when(plane < groups - 1)
            def _():
                def take(first):
                    part = near.at[:, :, pl.ds(first, snaps - first)]
                    remote(part, part, nz_send, nz_recv.at[0, 0], onward).wait_send()

                nz_do(take)


def near_list(group, tiles):
    return [2] if group == 4 and tiles > 4 else []


def on_device(owners, verts, features, tile_cols, tile_weights, graph_gain, graph_up, graph_down, lag_mix, time_gain, time_up, time_down):
    snaps, vert_dev, width = features.shape
    _, tiles, picks, tile, _ = tile_weights.shape
    layers, lags = lag_mix.shape[0], lag_mix.shape[1]
    group = -(-(lags - 1) // snaps)
    while owners % group or tile % (group * STRIP):
        group += 1
    rows = tile // group
    held = group * snaps
    near_count = len(near_list(group, tiles))
    apart, count = tiles - near_count, max(near_count, 1)
    bf16 = jnp.bfloat16
    dma = pltpu.SemaphoreType.DMA
    result = pl.pallas_call(
        functools.partial(kernel, owners, verts, group),
        out_shape=jax.ShapeDtypeStruct((snaps, tiles, tile, width), bf16),
        in_specs=[pl.BlockSpec(memory_space=pltpu.HBM)] * 10,
        out_specs=pl.BlockSpec(memory_space=pl.ANY),
        scratch_shapes=[pltpu.VMEM((snaps, verts * tiles, tile, width), bf16)] * layers + [
            pltpu.VMEM((snaps, tiles, picks, tile, tile), jnp.int32),
            pltpu.VMEM((snaps, tiles, tile, picks * tile), bf16),
            pltpu.VMEM((layers, apart, snaps, tile, width), bf16),
            pltpu.VMEM((layers, apart, 2 * held, rows, width), bf16),
            pltpu.VMEM((layers, apart, held, rows, width), bf16),
            pltpu.VMEM((layers, count, 3 * snaps, tile, width), bf16),
            pltpu.VMEM((layers, count, snaps, tile, width), bf16),
            pltpu.VMEM((layers, count, snaps, tile, width), bf16),
            pltpu.VMEM((count, snaps, tile, width), bf16),
            pltpu.VMEM(graph_up.shape, bf16),
            pltpu.VMEM(graph_down.shape, bf16),
            pltpu.VMEM(time_up.shape, bf16),
            pltpu.VMEM(time_down.shape, bf16),
            dma,
            dma((4,)),
            dma((tiles // 2 + 1,)),
            dma((verts - 1,)),
            dma((verts - 1,)),
            dma,
            dma((apart + min(EARLY, apart),)),
            dma((layers - 1, verts - 1)),
            dma((layers - 1, verts - 1)),
            dma,
            dma((layers, apart)),
            dma((layers,)),
            dma,
            dma(((layers - 1) * apart + 1,)),
            dma((layers - 1, verts - 1)),
            dma((layers - 1, verts - 1)),
            dma,
        ] + [dma, dma((layers, count))] * 3 + [
            dma,
            pltpu.SMEM(tile_cols.shape, jnp.int32),
            pltpu.VMEM(graph_gain.shape, jnp.float32),
            pltpu.VMEM(lag_mix.shape, jnp.float32),
            pltpu.VMEM(time_gain.shape, jnp.float32),
            dma((4,)),
        ],
        compiler_params=pltpu.CompilerParams(
            collective_id=0, has_side_effects=True, vmem_limit_bytes=36 * 1024 * 1024
        ),
    )(
        *[pltpu.with_memory_space_constraint(array, pltpu.HBM) for array in (
            features.reshape(snaps, tiles, tile, width), tile_cols, tile_weights,
            graph_gain, lag_mix, time_gain, graph_up, graph_down, time_up, time_down,
        )]
    )
    return result.reshape(features.shape)


def solution(mesh):
    return jax.shard_map(
        functools.partial(on_device, mesh.shape["snap"], mesh.shape["vert"]),
        mesh=mesh,
        in_specs=(
            P("snap", "vert", None),
            P("snap", "vert", None),
            P("snap", "vert", None, None, None),
        ) + (P(),) * 7,
        out_specs=P("snap", "vert", None),
        check_vma=False,
    )
```
